128 devices in a mesh: gx: 16 (over z, y), gy: 8 (over x, core).
Axes of the slice: x: 4, y: 4, z: 4, core: 2. Of those that a mesh axis runs over, the one named last changes fastest.
Arguments:
- rate_x: float32 [40, 128, 1024], P(None, 'gx', 'gy'), may hold values from 0.0025 to 0.25
- rate_y: float32 [40, 128, 1024], P(None, 'gx', 'gy'), may hold values from 0.00015625 to 0.015625
- land_mask: int32 [128, 1024], P('gx', 'gy'), may hold values 0 or 1
- obs_cell: int32 [128, 128, 32], P(('gx', 'gy')), may hold values from 0 to 81919
- obs_count: int32 [128, 128], P(('gx', 'gy')), may hold values from 0 to 32, as said below
- innovation: float32 [128, 128, 32], P(('gx', 'gy')), may hold values from -12 to 12
- obs_weight: float32 [128, 16, 256, 256], P(('gx', 'gy')), may hold values from -9 to 9, as said below
Outputs:
- solution: float32 [2, 40, 128, 1024], P(None, None, 'gx', 'gy')
- residual: float32 [2, 40, 128, 1024], P(None, None, 'gx', 'gy')
The draws below stay inside these ranges and needn't reach their ends.
Inputs may be any that keep to these rules, and one draw needn't show every extreme that they name: obs_count[s, d] slots of pair (s, d) hold observations, slots 0 to obs_count[s, d] - 1; in every draw some owner d has obs_count[s, d] = 32 for every source s. Each block obs_weight[s, n] is symmetric positive definite.
All inputs are finite; a program needn't handle non-finite values. No bound on the sum of `land_mask` on one device may be relied on, other than what follows from the above.
Results may differ from the reference program's by a relative error of at most 0.0003.
Values sent between devices are 32-bit elements; how exact they have to be, the bound alone decides.
No kernel may reach another device: no remote copies, remote signals or barrier semaphores. Data moves between devices by JAX's collectives and lax.ppermute only.
A program may use at most 128 MiB of HBM per device.

```python
import math
import jax
import jax.numpy as jnp
from jax import lax

TR = 2
LEV = 40
CX = 8
CY = 128
SLOTS = 32
RB = 256
ITERS = 2
NX = 128
NY = 1024
NODES = 128
NB = 16
CELLS_DEV = 81920
N_GX = 16
N_GY = 8


def draw_obs_count(key, part):
    first, second, third = jax.random.split(key, 3)
    base = jax.random.randint(first, (NODES, NODES), 0, SLOTS + 1)
    density = jax.random.randint(second, (1, NODES), 1, 5)
    full_owner = jax.random.randint(third, (), 0, NODES)
    counted = jnp.minimum(base * density // 2, SLOTS)
    owners = jnp.arange(NODES, dtype=jnp.int32)[None, :]
    return jnp.where(owners == full_owner, SLOTS, counted).astype(jnp.int32)


def draw_obs_weight(key, part):
    first, second = jax.random.split(key)
    spread = jnp.exp(jax.random.uniform(first, (NODES, NB, RB), jnp.float32, 0.0, math.log(3.0)))
    raw = jax.random.uniform(second, (NODES, NB, RB, RB), jnp.float32, -1.0, 1.0)
    symmetric = 0.5 * (raw + jnp.swapaxes(raw, 2, 3))
    identity = jnp.eye(RB, dtype=jnp.float32)
    inner_part = identity + 0.9 / (RB - 1) * symmetric * (1.0 - identity)
    return spread[:, :, :, None] * spread[:, :, None, :] * inner_part


def with_ends(drawn, rng, least, high):
    longest = drawn.shape.index(max(drawn.shape))
    spots = []
    for shift in (0, 1):
        where = [jax.random.randint(jax.random.fold_in(rng, axis), (), 0, length) for axis, length in enumerate(drawn.shape)]
        where[longest] = (where[longest] + shift) % drawn.shape[longest]
        spots.append(tuple(where))
    return drawn.at[spots[0]].set(least).at[spots[1]].set(high)


def block_levels(stream_key, extent, pieces, smallest, top_value):
    loudness, own = 1.0, jax.random.fold_in(stream_key, 6)
    for position, blocks in pieces:
        heights = jnp.exp(jax.random.uniform(jax.random.fold_in(own, position), (blocks,), jnp.float32, smallest / len(pieces), top_value / len(pieces)))
        loudness = loudness * jnp.repeat(heights, extent[position] // blocks).reshape([-1 if axis == position else 1 for axis in range(len(extent))])
    return loudness


def gaussian(own_key, shape, width, limit, shards=(), kind=jnp.bfloat16):
    array = width * jax.random.normal(own_key, shape, jnp.float32)
    if shards:
        array = array * block_levels(own_key, shape, shards, -0.22, 0.18)
    return jnp.clip(array, -limit, limit).astype(kind)


def setup_inputs(seed: int = 0) -> dict:
    seeds = jax.random.split(jax.random.key(seed), 8)
    return {
        "rate_x": jnp.clip(jnp.exp(math.log(0.25) - 4.6051702 * jax.random.uniform(seeds[0], (LEV, NX, NY), jnp.float32) ** block_levels(seeds[0], (LEV, NX, NY), ((1, 16), (2, 8)), -0.2, 0.2)), 0.0025, 0.25),
        "rate_y": jnp.clip(jnp.exp(math.log(0.015625) - 4.6051702 * jax.random.uniform(seeds[1], (LEV, NX, NY), jnp.float32) ** block_levels(seeds[1], (LEV, NX, NY), ((1, 16), (2, 8)), -0.2, 0.2)), 0.00015625, 0.015625),
        "land_mask": with_ends((jax.random.randint(seeds[2], (NX, NY), 0, 5) < 4).astype(jnp.int32), jax.random.fold_in(seeds[2], 1), 0, 1),
        "obs_cell": with_ends(jax.random.randint(seeds[3], (NODES, NODES, SLOTS), 0, CELLS_DEV), jax.random.fold_in(seeds[3], 1), 0, CELLS_DEV - 1).astype(jnp.int32),
        "obs_count": draw_obs_count(jax.random.fold_in(seeds[7], 71), 0),
        "innovation": gaussian(seeds[5], (NODES, NODES, SLOTS), 2.0, 12.0, ((0, 128),), jnp.float32),
        "obs_weight": draw_obs_weight(jax.random.fold_in(seeds[7], 71), 0),
    }


def compose_maps(earlier, following):
    return (earlier[0] * following[0], following[0] * earlier[1] + following[1])

def line_solve(state_field, decay_rate, line_axis, periodic):
    retention = jnp.broadcast_to(jnp.exp(-decay_rate), state_field.shape)
    one_minus = -jnp.expm1(-decay_rate)
    scaling = jnp.sqrt(one_minus * (1.0 + jnp.exp(-decay_rate)))
    weight = jnp.sqrt(jnp.sqrt(one_minus))
    line_length = state_field.shape[line_axis]
    factor, offset = lax.associative_scan(compose_maps, (retention, scaling * weight * state_field), axis=line_axis)
    if periodic:
        start_state = lax.index_in_dim(offset, line_length - 1, line_axis) / (1.0 - lax.index_in_dim(factor, line_length - 1, line_axis))
        forward = offset + factor * start_state
    else:
        forward = offset
    flipped = lax.associative_scan(compose_maps, (jnp.flip(retention, line_axis), jnp.flip(retention * forward, line_axis)), axis=line_axis)
    back_factor = jnp.flip(flipped[0], line_axis)
    back_offset = jnp.flip(flipped[1], line_axis)
    next_factor = jnp.concatenate([lax.slice_in_dim(back_factor, 1, line_length, axis=line_axis), jnp.ones_like(lax.slice_in_dim(back_factor, 0, 1, axis=line_axis))], axis=line_axis)
    next_offset = jnp.concatenate([lax.slice_in_dim(back_offset, 1, line_length, axis=line_axis), jnp.zeros_like(lax.slice_in_dim(back_offset, 0, 1, axis=line_axis))], axis=line_axis)
    if periodic:
        entering = lax.index_in_dim(back_offset, 0, line_axis) / (1.0 - lax.index_in_dim(back_factor, 0, line_axis))
        later_part = next_offset + next_factor * entering
    else:
        later_part = next_offset
    return weight * scaling * (forward + later_part)

def to_blocks(state_field):
    shaped = state_field.reshape(TR, LEV, N_GX, CX, N_GY, CY).transpose(2, 4, 0, 1, 3, 5)
    return shaped.reshape(NODES, CELLS_DEV)

def from_blocks(owned):
    shaped = owned.reshape(N_GX, N_GY, TR, LEV, CX, CY).transpose(2, 3, 0, 4, 1, 5)
    return shaped.reshape(TR, LEV, NX, NY)

def reference(rate_x, rate_y, land_mask, obs_cell, obs_count, innovation, obs_weight):
    ocean = land_mask.astype(jnp.float32)

    def spread(vector):
        return ocean * line_solve(line_solve(ocean * vector, rate_x, 2, True), rate_y, 3, False)

    def gather_back(vector):
        return ocean * line_solve(line_solve(ocean * vector, rate_y, 3, False), rate_x, 2, True)
    occupied = (jnp.arange(SLOTS, dtype=jnp.int32)[None, None, :] < obs_count[:, :, None]).astype(jnp.float32)
    cell_index = obs_cell.reshape(NODES, NODES * SLOTS).astype(jnp.int32)

    def weigh_obs(values):
        packed = (occupied * values).reshape(NODES, NB, RB)
        mixed = jnp.einsum('snij,snj->sni', obs_weight, packed, precision=lax.Precision.HIGHEST)
        return occupied * mixed.reshape(NODES, NODES, SLOTS)

    def observe(vector):
        picked = jnp.take_along_axis(to_blocks(vector), cell_index, axis=1).reshape(NODES, NODES, SLOTS)
        return jnp.transpose(picked, (1, 0, 2))

    def deposit(values):
        owner_view = jnp.transpose(values, (1, 0, 2)).reshape(NODES, NODES * SLOTS)

        def add_block(positions, amounts):
            return jnp.zeros((CELLS_DEV,), jnp.float32).at[positions].add(amounts)
        return from_blocks(jax.vmap(add_block)(cell_index, owner_view))
    right_side = gather_back(deposit(weigh_obs(innovation)))
    solution = jnp.zeros_like(right_side)
    residual = right_side
    direction = right_side
    norm_now = jnp.sum(residual * residual)
    for iteration in range(ITERS):
        hessian_dir = direction + gather_back(deposit(weigh_obs(observe(spread(direction)))))
        step_length = norm_now / jnp.sum(direction * hessian_dir)
        solution = solution + step_length * direction
        residual = residual - step_length * hessian_dir
        norm_next = jnp.sum(residual * residual)
        direction = residual + norm_next / norm_now * direction
        norm_now = norm_next
    return (solution, residual)
```

```python
import jax
import jax.numpy as jnp
from jax import lax
from jax.sharding import PartitionSpec as P

TR = 2
ITERS = 2


def shift_along(values, distance, line_axis, reverse, filler):
    length = values.shape[line_axis]
    edge_shape = list(values.shape)
    edge_shape[line_axis] = distance
    edge = jnp.full(tuple(edge_shape), filler, values.dtype)
    if reverse:
        return jnp.concatenate(
            [lax.slice_in_dim(values, distance, length, axis=line_axis), edge], axis=line_axis
        )
    return jnp.concatenate(
        [edge, lax.slice_in_dim(values, 0, length - distance, axis=line_axis)], axis=line_axis
    )


def factor_levels(retention, line_axis, reverse):
    length = retention.shape[line_axis]
    stored = []
    factor = retention
    distance = 1
    while distance < length:
        stored.append(factor)
        factor = factor * shift_along(factor, distance, line_axis, reverse, 1.0)
        distance = distance * 2
    return (stored, factor)


def scan_offsets(stored, forcing, line_axis, reverse):
    distance = 1
    for level_factor in stored:
        forcing = forcing + level_factor * shift_along(forcing, distance, line_axis, reverse, 0.0)
        distance = distance * 2
    return forcing


def make_plan(decay_rate, line_axis, axis_name, periodic):
    retention = jnp.exp(-decay_rate)[None]
    one_minus = -jnp.expm1(-decay_rate)
    scaling = jnp.sqrt(one_minus * (1.0 + jnp.exp(-decay_rate)))
    weight = jnp.sqrt(jnp.sqrt(one_minus))
    length = retention.shape[line_axis]
    forward_stored, prefix = factor_levels(retention, line_axis, False)
    backward_stored, suffix = factor_levels(retention, line_axis, True)
    back_of_prefix = scan_offsets(backward_stored, retention * prefix, line_axis, True)
    totals = jnp.stack(
        [
            lax.index_in_dim(prefix, length - 1, line_axis, keepdims=False),
            lax.index_in_dim(suffix, 0, line_axis, keepdims=False),
            lax.index_in_dim(back_of_prefix, 0, line_axis, keepdims=False),
        ]
    )
    return dict(
        retention=retention,
        gain=scaling * weight,
        gain_out=weight * scaling,
        forward_stored=forward_stored,
        backward_stored=backward_stored,
        prefix=prefix,
        suffix=suffix,
        back_of_prefix=back_of_prefix,
        rate_totals=lax.all_gather(totals, axis_name),
        axis_name=axis_name,
        periodic=periodic,
        line_axis=line_axis,
    )


def carries(got, rate_totals, periodic, axis_name):
    count = got.shape[0]
    offsets = [got[k, 0] for k in range(count)]
    back_parts = [got[k, 1] for k in range(count)]
    factors = [rate_totals[k, 0] for k in range(count)]
    back_factors = [rate_totals[k, 1] for k in range(count)]
    back_gains = [rate_totals[k, 2] for k in range(count)]
    if periodic:
        total = offsets[0]
        product = factors[0]
        for k in range(1, count):
            total = factors[k] * total + offsets[k]
            product = product * factors[k]
        first = total / (1.0 - product)
    else:
        first = jnp.zeros_like(offsets[0])
    entering = [first]
    for k in range(count - 1):
        entering.append(offsets[k] + factors[k] * entering[k])
    back_totals = [back_parts[k] + entering[k] * back_gains[k] for k in range(count)]
    if periodic:
        total = back_totals[count - 1]
        product = back_factors[count - 1]
        for k in range(count - 2, -1, -1):
            total = back_totals[k] + back_factors[k] * total
            product = product * back_factors[k]
        last = total / (1.0 - product)
    else:
        last = jnp.zeros_like(offsets[0])
    leaving = [None] * count
    leaving[count - 1] = last
    for k in range(count - 2, -1, -1):
        leaving[k] = back_totals[k + 1] + back_factors[k + 1] * leaving[k + 1]
    place = lax.axis_index(axis_name)
    mine_in = lax.dynamic_index_in_dim(jnp.stack(entering), place, 0, False)
    mine_out = lax.dynamic_index_in_dim(jnp.stack(leaving), place, 0, False)
    return mine_in, mine_out


def line_operator(state_field, plan):
    line_axis = plan["line_axis"]
    length = state_field.shape[line_axis]
    offset = scan_offsets(plan["forward_stored"], plan["gain"] * state_field, line_axis, False)
    back_offset = scan_offsets(
        plan["backward_stored"], plan["retention"] * offset, line_axis, True
    )
    mine = jnp.stack(
        [
            lax.index_in_dim(offset, length - 1, line_axis, keepdims=False),
            lax.index_in_dim(back_offset, 0, line_axis, keepdims=False),
        ]
    )
    got = lax.all_gather(mine, plan["axis_name"])
    entering, leaving = carries(got, plan["rate_totals"], plan["periodic"], plan["axis_name"])
    entering = jnp.expand_dims(entering, line_axis)
    leaving = jnp.expand_dims(leaving, line_axis)
    forward = offset + plan["prefix"] * entering
    back_offset = back_offset + entering * plan["back_of_prefix"]
    next_factor = shift_along(plan["suffix"], 1, line_axis, True, 1.0)
    next_offset = shift_along(back_offset, 1, line_axis, True, 0.0)
    return plan["gain_out"] * (forward + next_offset + next_factor * leaving)


def global_dot(first_field, second_field):
    return lax.psum(jnp.sum(first_field * second_field), ("gx", "gy"))


def on_device(rate_x, rate_y, land_mask, obs_cell, obs_count, innovation, obs_weight):
    ocean = land_mask.astype(jnp.float32)
    field_shape = (TR,) + rate_x.shape
    plan_along_x = make_plan(rate_x, 2, "gx", True)
    plan_along_y = make_plan(rate_y, 3, "gy", False)

    def along_x(state_field):
        return line_operator(state_field, plan_along_x)

    def along_y(state_field):
        return line_operator(state_field, plan_along_y)

    def gather_back(vector):
        return ocean * along_x(along_y(ocean * vector))

    cell_index = obs_cell[0]
    occupied = (
        lax.broadcasted_iota(jnp.int32, cell_index.shape, 1) < obs_count[0][:, None]
    ).astype(jnp.float32)
    blocks = obs_weight[0]

    def weigh_obs(values):
        packed = (occupied * values).reshape(blocks.shape[0], blocks.shape[1])
        mixed = jnp.einsum("nij,nj->ni", blocks, packed, precision=lax.Precision.HIGHEST)
        return occupied * mixed.reshape(occupied.shape)

    def deposit(values):
        arrived = lax.all_to_all(values, ("gx", "gy"), split_axis=0, concat_axis=0, tiled=True)
        flat_cells = (
            jnp.zeros((TR * rate_x.size,), jnp.float32)
            .at[cell_index.reshape(-1)]
            .add(arrived.reshape(-1))
        )
        return flat_cells.reshape(field_shape)

    right_side = gather_back(deposit(weigh_obs(innovation[0])))
    solution = jnp.zeros_like(right_side)
    residual = right_side
    direction = right_side
    norm_now = global_dot(residual, residual)
    for iteration in range(ITERS):
        picked = jnp.take(
            (ocean * along_y(along_x(ocean * direction))).reshape(-1),
            cell_index.reshape(-1),
            axis=0,
        ).reshape(cell_index.shape)
        hessian_dir = direction + gather_back(
            deposit(
                weigh_obs(
                    lax.all_to_all(picked, ("gx", "gy"), split_axis=0, concat_axis=0, tiled=True)
                )
            )
        )
        step_length = norm_now / global_dot(direction, hessian_dir)
        solution = solution + step_length * direction
        residual = residual - step_length * hessian_dir
        norm_next = global_dot(residual, residual)
        direction = residual + norm_next / norm_now * direction
        norm_now = norm_next
    return (solution, residual)


def solution(mesh):
    placed = (
        P(None, "gx", "gy"),
        P(None, "gx", "gy"),
        P("gx", "gy"),
        P(("gx", "gy"), None, None),
        P(("gx", "gy"), None),
        P(("gx", "gy"), None, None),
        P(("gx", "gy"), None, None, None),
    )
    return jax.shard_map(
        on_device,
        mesh=mesh,
        in_specs=placed,
        out_specs=(P(None, None, "gx", "gy"), P(None, None, "gx", "gy")),
        check_vma=False,
    )
```

```python
import jax
import jax.numpy as jnp
from jax import lax
from jax.sharding import PartitionSpec as P

TR = 2
ITERS = 2


def shift_along(values, distance, line_axis, reverse, filler):
    length = values.shape[line_axis]
    edge_shape = list(values.shape)
    edge_shape[line_axis] = distance
    edge = jnp.full(tuple(edge_shape), filler, values.dtype)
    if reverse:
        return jnp.concatenate(
            [lax.slice_in_dim(values, distance, length, axis=line_axis), edge], axis=line_axis
        )
    return jnp.concatenate(
        [edge, lax.slice_in_dim(values, 0, length - distance, axis=line_axis)], axis=line_axis
    )


def factor_levels(retention, line_axis, reverse):
    length = retention.shape[line_axis]
    stored = []
    factor = retention
    distance = 1
    while distance < length:
        stored.append(factor)
        factor = factor * shift_along(factor, distance, line_axis, reverse, 1.0)
        distance = distance * 2
    return (stored, factor)


def scan_offsets(stored, forcing, line_axis, reverse):
    distance = 1
    for level_factor in stored:
        forcing = forcing + level_factor * shift_along(forcing, distance, line_axis, reverse, 0.0)
        distance = distance * 2
    return forcing


def make_plan(decay_rate, line_axis, axis_name, periodic):
    retention = jnp.exp(-decay_rate)[None]
    one_minus = -jnp.expm1(-decay_rate)
    scaling = jnp.sqrt(one_minus * (1.0 + jnp.exp(-decay_rate)))
    weight = jnp.sqrt(jnp.sqrt(one_minus))
    length = retention.shape[line_axis]
    forward_stored, prefix = factor_levels(retention, line_axis, False)
    backward_stored, suffix = factor_levels(retention, line_axis, True)
    back_of_prefix = scan_offsets(backward_stored, retention * prefix, line_axis, True)
    totals = jnp.stack(
        [
            lax.index_in_dim(prefix, length - 1, line_axis, keepdims=False),
            lax.index_in_dim(suffix, 0, line_axis, keepdims=False),
            lax.index_in_dim(back_of_prefix, 0, line_axis, keepdims=False),
        ]
    )
    return dict(
        retention=retention,
        gain=scaling * weight,
        gain_out=weight * scaling,
        forward_stored=forward_stored,
        backward_stored=backward_stored,
        prefix=prefix,
        suffix=suffix,
        back_of_prefix=back_of_prefix,
        rate_totals=lax.all_gather(totals, axis_name),
        axis_name=axis_name,
        periodic=periodic,
        line_axis=line_axis,
    )


def carries(got, rate_totals, periodic, axis_name):
    count = got.shape[0]
    offsets = [got[k, 0] for k in range(count)]
    back_parts = [got[k, 1] for k in range(count)]
    factors = [rate_totals[k, 0] for k in range(count)]
    back_factors = [rate_totals[k, 1] for k in range(count)]
    back_gains = [rate_totals[k, 2] for k in range(count)]
    if periodic:
        total = offsets[0]
        product = factors[0]
        for k in range(1, count):
            total = factors[k] * total + offsets[k]
            product = product * factors[k]
        first = total / (1.0 - product)
    else:
        first = jnp.zeros_like(offsets[0])
    entering = [first]
    for k in range(count - 1):
        entering.append(offsets[k] + factors[k] * entering[k])
    back_totals = [back_parts[k] + entering[k] * back_gains[k] for k in range(count)]
    if periodic:
        total = back_totals[count - 1]
        product = back_factors[count - 1]
        for k in range(count - 2, -1, -1):
            total = back_totals[k] + back_factors[k] * total
            product = product * back_factors[k]
        last = total / (1.0 - product)
    else:
        last = jnp.zeros_like(offsets[0])
    leaving = [None] * count
    leaving[count - 1] = last
    for k in range(count - 2, -1, -1):
        leaving[k] = back_totals[k + 1] + back_factors[k + 1] * leaving[k + 1]
    place = lax.axis_index(axis_name)
    mine_in = lax.dynamic_index_in_dim(jnp.stack(entering), place, 0, False)
    mine_out = lax.dynamic_index_in_dim(jnp.stack(leaving), place, 0, False)
    return mine_in, mine_out


def line_operator(state_field, plan):
    line_axis = plan["line_axis"]
    length = state_field.shape[line_axis]
    offset = scan_offsets(plan["forward_stored"], plan["gain"] * state_field, line_axis, False)
    back_offset = scan_offsets(
        plan["backward_stored"], plan["retention"] * offset, line_axis, True
    )
    mine = jnp.stack(
        [
            lax.index_in_dim(offset, length - 1, line_axis, keepdims=False),
            lax.index_in_dim(back_offset, 0, line_axis, keepdims=False),
        ]
    )
    got = lax.all_gather(mine, plan["axis_name"])
    entering, leaving = carries(got, plan["rate_totals"], plan["periodic"], plan["axis_name"])
    entering = jnp.expand_dims(entering, line_axis)
    leaving = jnp.expand_dims(leaving, line_axis)
    forward = offset + plan["prefix"] * entering
    back_offset = back_offset + entering * plan["back_of_prefix"]
    next_factor = shift_along(plan["suffix"], 1, line_axis, True, 1.0)
    next_offset = shift_along(back_offset, 1, line_axis, True, 0.0)
    return plan["gain_out"] * (forward + next_offset + next_factor * leaving)


def exchange(values, partial):
    rows = values.shape[0]
    packed = jnp.concatenate(
        [values, jnp.broadcast_to(partial.astype(values.dtype), (rows, 1))], axis=1
    )
    arrived = lax.all_to_all(packed, ("gx", "gy"), split_axis=0, concat_axis=0, tiled=True)
    return arrived[:, :-1], jnp.sum(arrived[:, -1])


def on_device(rate_x, rate_y, land_mask, obs_cell, obs_count, innovation, obs_weight):
    ocean = land_mask.astype(jnp.float32)
    field_shape = (TR,) + rate_x.shape
    plan_along_x = make_plan(rate_x, 2, "gx", True)
    plan_along_y = make_plan(rate_y, 3, "gy", False)

    def along_x(state_field):
        return line_operator(state_field, plan_along_x)

    def along_y(state_field):
        return line_operator(state_field, plan_along_y)

    def spread(vector):
        return ocean * along_y(along_x(ocean * vector))

    def gather_back(vector):
        return ocean * along_x(along_y(ocean * vector))

    cell_index = obs_cell[0]
    occupied = (
        lax.broadcasted_iota(jnp.int32, cell_index.shape, 1) < obs_count[0][:, None]
    ).astype(jnp.float32)
    blocks = obs_weight[0]

    def weigh_obs(values):
        packed = (occupied * values).reshape(blocks.shape[0], blocks.shape[1])
        mixed = jnp.einsum("nij,nj->ni", blocks, packed, precision=lax.Precision.HIGHEST)
        return occupied * mixed.reshape(occupied.shape)

    def deposit_local(arrived):
        flat_cells = (
            jnp.zeros((TR * rate_x.size,), jnp.float32)
            .at[cell_index.reshape(-1)]
            .add(arrived.reshape(-1))
        )
        return flat_cells.reshape(field_shape)

    def observe(vector):
        return jnp.take(vector.reshape(-1), cell_index.reshape(-1), axis=0).reshape(
            cell_index.shape
        )

    weighted = weigh_obs(innovation[0])
    arrived = lax.all_to_all(weighted, ("gx", "gy"), split_axis=0, concat_axis=0, tiled=True)
    right_side = gather_back(deposit_local(arrived))
    solution = jnp.zeros_like(right_side)
    residual = right_side
    direction = right_side
    norm_now = None
    previous_seen = None
    for iteration in range(ITERS):
        seen, norm_next = exchange(observe(spread(residual)), jnp.sum(residual * residual))
        if iteration == 0:
            direction = residual
        else:
            ratio = norm_next / norm_now
            seen = seen + ratio * previous_seen
            direction = residual + ratio * direction
        norm_now = norm_next
        mixed = weigh_obs(seen)
        returned, curvature = exchange(
            mixed, jnp.sum(direction * direction) + jnp.sum(seen * mixed)
        )
        hessian_dir = direction + gather_back(deposit_local(returned))
        step_length = norm_now / curvature
        solution = solution + step_length * direction
        residual = residual - step_length * hessian_dir
        previous_seen = seen
    return (solution, residual)


def solution(mesh):
    placed = (
        P(None, "gx", "gy"),
        P(None, "gx", "gy"),
        P("gx", "gy"),
        P(("gx", "gy"), None, None),
        P(("gx", "gy"), None),
        P(("gx", "gy"), None, None),
        P(("gx", "gy"), None, None, None),
    )
    return jax.shard_map(
        on_device,
        mesh=mesh,
        in_specs=placed,
        out_specs=(P(None, None, "gx", "gy"), P(None, None, "gx", "gy")),
        check_vma=False,
    )
```

```python
import jax
import jax.numpy as jnp
from jax import lax
from jax.sharding import PartitionSpec as P

TR = 2
ITERS = 2


def shift_along(values, distance, line_axis, reverse, filler):
    length = values.shape[line_axis]
    edge_shape = list(values.shape)
    edge_shape[line_axis] = distance
    edge = jnp.full(tuple(edge_shape), filler, values.dtype)
    if reverse:
        return jnp.concatenate(
            [lax.slice_in_dim(values, distance, length, axis=line_axis), edge], axis=line_axis
        )
    return jnp.concatenate(
        [edge, lax.slice_in_dim(values, 0, length - distance, axis=line_axis)], axis=line_axis
    )


def factor_levels(retention, line_axis, reverse):
    length = retention.shape[line_axis]
    stored = []
    factor = retention
    distance = 1
    while distance < length:
        stored.append(factor)
        factor = factor * shift_along(factor, distance, line_axis, reverse, 1.0)
        distance = distance * 2
    return (stored, factor)


def scan_offsets(stored, forcing, line_axis, reverse):
    distance = 1
    for level_factor in stored:
        forcing = forcing + level_factor * shift_along(forcing, distance, line_axis, reverse, 0.0)
        distance = distance * 2
    return forcing


def make_plan(decay_rate, line_axis, axis_name, periodic):
    retention = jnp.exp(-decay_rate)[None]
    one_minus = -jnp.expm1(-decay_rate)
    scaling = jnp.sqrt(one_minus * (1.0 + jnp.exp(-decay_rate)))
    weight = jnp.sqrt(jnp.sqrt(one_minus))
    length = retention.shape[line_axis]
    forward_stored, prefix = factor_levels(retention, line_axis, False)
    backward_stored, suffix = factor_levels(retention, line_axis, True)
    back_of_prefix = scan_offsets(backward_stored, retention * prefix, line_axis, True)
    totals = jnp.stack(
        [
            lax.index_in_dim(prefix, length - 1, line_axis, keepdims=False),
            lax.index_in_dim(suffix, 0, line_axis, keepdims=False),
            lax.index_in_dim(back_of_prefix, 0, line_axis, keepdims=False),
        ]
    )
    return dict(
        retention=retention,
        gain=scaling * weight,
        gain_out=weight * scaling,
        forward_stored=forward_stored,
        backward_stored=backward_stored,
        prefix=prefix,
        suffix=suffix,
        back_of_prefix=back_of_prefix,
        rate_totals=lax.all_gather(totals, axis_name),
        axis_name=axis_name,
        periodic=periodic,
        line_axis=line_axis,
    )


def carries(got, rate_totals, periodic, axis_name):
    count = got.shape[0]
    offsets = [got[k, 0] for k in range(count)]
    back_parts = [got[k, 1] for k in range(count)]
    factors = [rate_totals[k, 0] for k in range(count)]
    back_factors = [rate_totals[k, 1] for k in range(count)]
    back_gains = [rate_totals[k, 2] for k in range(count)]
    if periodic:
        total = offsets[0]
        product = factors[0]
        for k in range(1, count):
            total = factors[k] * total + offsets[k]
            product = product * factors[k]
        first = total / (1.0 - product)
    else:
        first = jnp.zeros_like(offsets[0])
    entering = [first]
    for k in range(count - 1):
        entering.append(offsets[k] + factors[k] * entering[k])
    back_totals = [back_parts[k] + entering[k] * back_gains[k] for k in range(count)]
    if periodic:
        total = back_totals[count - 1]
        product = back_factors[count - 1]
        for k in range(count - 2, -1, -1):
            total = back_totals[k] + back_factors[k] * total
            product = product * back_factors[k]
        last = total / (1.0 - product)
    else:
        last = jnp.zeros_like(offsets[0])
    leaving = [None] * count
    leaving[count - 1] = last
    for k in range(count - 2, -1, -1):
        leaving[k] = back_totals[k + 1] + back_factors[k + 1] * leaving[k + 1]
    place = lax.axis_index(axis_name)
    mine_in = entering[0]
    mine_out = leaving[0]
    for k in range(1, count):
        mine_in = jnp.where(place == k, entering[k], mine_in)
        mine_out = jnp.where(place == k, leaving[k], mine_out)
    return mine_in, mine_out


def line_operator(state_field, plan):
    line_axis = plan["line_axis"]
    length = state_field.shape[line_axis]
    offset = scan_offsets(plan["forward_stored"], plan["gain"] * state_field, line_axis, False)
    back_offset = scan_offsets(
        plan["backward_stored"], plan["retention"] * offset, line_axis, True
    )
    mine = jnp.stack(
        [
            lax.index_in_dim(offset, length - 1, line_axis, keepdims=False),
            lax.index_in_dim(back_offset, 0, line_axis, keepdims=False),
        ]
    )
    got = lax.all_gather(mine, plan["axis_name"])
    entering, leaving = carries(got, plan["rate_totals"], plan["periodic"], plan["axis_name"])
    entering = jnp.expand_dims(entering, line_axis)
    leaving = jnp.expand_dims(leaving, line_axis)
    forward = offset + plan["prefix"] * entering
    back_offset = back_offset + entering * plan["back_of_prefix"]
    next_factor = shift_along(plan["suffix"], 1, line_axis, True, 1.0)
    next_offset = shift_along(back_offset, 1, line_axis, True, 0.0)
    return plan["gain_out"] * (forward + next_offset + next_factor * leaving)


def exchange(values, partial):
    rows = values.shape[0]
    packed = jnp.concatenate(
        [values, jnp.broadcast_to(partial.astype(values.dtype), (rows, 1))], axis=1
    )
    arrived = lax.all_to_all(packed, ("gx", "gy"), split_axis=0, concat_axis=0, tiled=True)
    return arrived[:, :-1], jnp.sum(arrived[:, -1])


def on_device(rate_x, rate_y, land_mask, obs_cell, obs_count, innovation, obs_weight):
    ocean = land_mask.astype(jnp.float32)
    field_shape = (TR,) + rate_x.shape
    plan_along_x = make_plan(rate_x, 2, "gx", True)
    plan_along_y = make_plan(rate_y, 3, "gy", False)

    def along_x(state_field):
        return line_operator(state_field, plan_along_x)

    def along_y(state_field):
        return line_operator(state_field, plan_along_y)

    def spread(vector):
        return ocean * along_y(along_x(ocean * vector))

    def gather_back(vector):
        return ocean * along_x(along_y(ocean * vector))

    cell_index = obs_cell[0]
    occupied = (
        lax.broadcasted_iota(jnp.int32, cell_index.shape, 1) < obs_count[0][:, None]
    ).astype(jnp.float32)
    blocks = obs_weight[0]

    def weigh_obs(values):
        packed = (occupied * values).reshape(blocks.shape[0], blocks.shape[1])
        mixed = jnp.einsum("nij,nj->ni", blocks, packed, precision=lax.Precision.HIGHEST)
        return occupied * mixed.reshape(occupied.shape)

    lanes = field_shape[-1]
    rows = TR * rate_x.size // lanes
    flat_index = cell_index.reshape(-1)
    row_hot = (
        (flat_index // lanes)[:, None] == lax.broadcasted_iota(jnp.int32, (1, rows), 1)
    ).astype(jnp.float32)
    lane_hot = (
        (flat_index % lanes)[:, None] == lax.broadcasted_iota(jnp.int32, (1, lanes), 1)
    ).astype(jnp.float32)

    def deposit_local(arrived):
        spread_lanes = arrived.reshape(-1, 1) * lane_hot
        cells = lax.dot_general(
            row_hot,
            spread_lanes,
            (((0,), (0,)), ((), ())),
            precision=lax.Precision.HIGHEST,
            preferred_element_type=jnp.float32,
        )
        return cells.reshape(field_shape)

    def observe(vector):
        picked_rows = jnp.dot(
            row_hot,
            vector.reshape(rows, lanes),
            precision=lax.Precision.HIGHEST,
            preferred_element_type=jnp.float32,
        )
        return jnp.sum(picked_rows * lane_hot, axis=1).reshape(cell_index.shape)

    weighted = weigh_obs(innovation[0])
    arrived = lax.all_to_all(weighted, ("gx", "gy"), split_axis=0, concat_axis=0, tiled=True)
    right_side = gather_back(deposit_local(arrived))
    solution = jnp.zeros_like(right_side)
    residual = right_side
    direction = right_side
    norm_now = None
    previous_seen = None
    for iteration in range(ITERS):
        seen, norm_next = exchange(observe(spread(residual)), jnp.sum(residual * residual))
        if iteration == 0:
            direction = residual
        else:
            ratio = norm_next / norm_now
            seen = seen + ratio * previous_seen
            direction = residual + ratio * direction
        norm_now = norm_next
        mixed = weigh_obs(seen)
        returned, curvature = exchange(
            mixed, jnp.sum(direction * direction) + jnp.sum(seen * mixed)
        )
        hessian_dir = direction + gather_back(deposit_local(returned))
        step_length = norm_now / curvature
        solution = solution + step_length * direction
        residual = residual - step_length * hessian_dir
        previous_seen = seen
    return (solution, residual)


def solution(mesh):
    placed = (
        P(None, "gx", "gy"),
        P(None, "gx", "gy"),
        P("gx", "gy"),
        P(("gx", "gy"), None, None),
        P(("gx", "gy"), None),
        P(("gx", "gy"), None, None),
        P(("gx", "gy"), None, None, None),
    )
    return jax.shard_map(
        on_device,
        mesh=mesh,
        in_specs=placed,
        out_specs=(P(None, None, "gx", "gy"), P(None, None, "gx", "gy")),
        check_vma=False,
    )
```

```python
import jax
import jax.numpy as jnp
from jax import lax
from jax.sharding import PartitionSpec as P
from jax.experimental import pallas as pl
from jax.experimental.pallas import tpu as pltpu

TR = 2
ITERS = 2


def shift_along(values, distance, line_axis, reverse, filler):
    length = values.shape[line_axis]
    edge_shape = list(values.shape)
    edge_shape[line_axis] = distance
    edge = jnp.full(tuple(edge_shape), filler, values.dtype)
    if reverse:
        return jnp.concatenate(
            [lax.slice_in_dim(values, distance, length, axis=line_axis), edge], axis=line_axis
        )
    return jnp.concatenate(
        [edge, lax.slice_in_dim(values, 0, length - distance, axis=line_axis)], axis=line_axis
    )


def factor_levels(retention, line_axis, reverse):
    length = retention.shape[line_axis]
    stored = []
    factor = retention
    distance = 1
    while distance < length:
        stored.append(factor)
        factor = factor * shift_along(factor, distance, line_axis, reverse, 1.0)
        distance = distance * 2
    return (stored, factor)


def scan_offsets(stored, forcing, line_axis, reverse):
    distance = 1
    for level_factor in stored:
        forcing = forcing + level_factor * shift_along(forcing, distance, line_axis, reverse, 0.0)
        distance = distance * 2
    return forcing


def make_plan(decay_rate, line_axis, axis_name, periodic):
    retention = jnp.exp(-decay_rate)[None]
    one_minus = -jnp.expm1(-decay_rate)
    scaling = jnp.sqrt(one_minus * (1.0 + jnp.exp(-decay_rate)))
    weight = jnp.sqrt(jnp.sqrt(one_minus))
    length = retention.shape[line_axis]
    forward_stored, prefix = factor_levels(retention, line_axis, False)
    backward_stored, suffix = factor_levels(retention, line_axis, True)
    back_of_prefix = scan_offsets(backward_stored, retention * prefix, line_axis, True)
    totals = jnp.stack(
        [
            lax.index_in_dim(prefix, length - 1, line_axis, keepdims=False),
            lax.index_in_dim(suffix, 0, line_axis, keepdims=False),
            lax.index_in_dim(back_of_prefix, 0, line_axis, keepdims=False),
        ]
    )
    return dict(
        retention=retention,
        gain=scaling * weight,
        gain_out=weight * scaling,
        forward_stored=forward_stored,
        backward_stored=backward_stored,
        prefix=prefix,
        suffix=suffix,
        back_of_prefix=back_of_prefix,
        rate_totals=lax.all_gather(totals, axis_name),
        axis_name=axis_name,
        periodic=periodic,
        line_axis=line_axis,
    )


def carries(got, rate_totals, periodic, axis_name):
    count = got.shape[0]
    offsets = [got[k, 0] for k in range(count)]
    back_parts = [got[k, 1] for k in range(count)]
    factors = [rate_totals[k, 0] for k in range(count)]
    back_factors = [rate_totals[k, 1] for k in range(count)]
    back_gains = [rate_totals[k, 2] for k in range(count)]
    if periodic:
        total = offsets[0]
        product = factors[0]
        for k in range(1, count):
            total = factors[k] * total + offsets[k]
            product = product * factors[k]
        first = total / (1.0 - product)
    else:
        first = jnp.zeros_like(offsets[0])
    entering = [first]
    for k in range(count - 1):
        entering.append(offsets[k] + factors[k] * entering[k])
    back_totals = [back_parts[k] + entering[k] * back_gains[k] for k in range(count)]
    if periodic:
        total = back_totals[count - 1]
        product = back_factors[count - 1]
        for k in range(count - 2, -1, -1):
            total = back_totals[k] + back_factors[k] * total
            product = product * back_factors[k]
        last = total / (1.0 - product)
    else:
        last = jnp.zeros_like(offsets[0])
    leaving = [None] * count
    leaving[count - 1] = last
    for k in range(count - 2, -1, -1):
        leaving[k] = back_totals[k + 1] + back_factors[k + 1] * leaving[k + 1]
    place = lax.axis_index(axis_name)
    mine_in = lax.dynamic_index_in_dim(jnp.stack(entering), place, 0, False)
    mine_out = lax.dynamic_index_in_dim(jnp.stack(leaving), place, 0, False)
    return mine_in, mine_out


def line_operator(state_field, plan):
    line_axis = plan["line_axis"]
    length = state_field.shape[line_axis]
    offset = scan_offsets(plan["forward_stored"], plan["gain"] * state_field, line_axis, False)
    back_offset = scan_offsets(
        plan["backward_stored"], plan["retention"] * offset, line_axis, True
    )
    mine = jnp.stack(
        [
            lax.index_in_dim(offset, length - 1, line_axis, keepdims=False),
            lax.index_in_dim(back_offset, 0, line_axis, keepdims=False),
        ]
    )
    got = lax.all_gather(mine, plan["axis_name"])
    entering, leaving = carries(got, plan["rate_totals"], plan["periodic"], plan["axis_name"])
    entering = jnp.expand_dims(entering, line_axis)
    leaving = jnp.expand_dims(leaving, line_axis)
    forward = offset + plan["prefix"] * entering
    back_offset = back_offset + entering * plan["back_of_prefix"]
    next_factor = shift_along(plan["suffix"], 1, line_axis, True, 1.0)
    next_offset = shift_along(back_offset, 1, line_axis, True, 0.0)
    return plan["gain_out"] * (forward + next_offset + next_factor * leaving)


CHUNK = 512


def split_three(values):
    high = values.astype(jnp.bfloat16)
    rest = values - high.astype(jnp.float32)
    middle = rest.astype(jnp.bfloat16)
    low = (rest - middle.astype(jnp.float32)).astype(jnp.bfloat16)
    return high, middle, low


def pick_kernel(field_ref, rows_ref, lanes_ref, out_ref):
    field_rows, lanes = field_ref.shape
    chunk = rows_ref.shape[1]
    parts = split_three(field_ref[...].T)
    hot = (
        lax.broadcasted_iota(jnp.int32, (field_rows, chunk), 0) == rows_ref[...]
    ).astype(jnp.bfloat16)
    picked = None
    for part in parts:
        term = jnp.dot(part, hot, preferred_element_type=jnp.float32)
        picked = term if picked is None else picked + term
    chosen = lax.broadcasted_iota(jnp.int32, (lanes, chunk), 0) == lanes_ref[...]
    out_ref[...] = jnp.sum(jnp.where(chosen, picked, 0.0), axis=0, keepdims=True)


def pick_cells(field_rows, rows, lanes):
    count = rows.shape[1]
    return pl.pallas_call(
        pick_kernel,
        out_shape=jax.ShapeDtypeStruct((1, count), jnp.float32),
        grid=(count // CHUNK,),
        in_specs=[
            pl.BlockSpec(field_rows.shape, lambda i: (0, 0)),
            pl.BlockSpec((1, CHUNK), lambda i: (0, i)),
            pl.BlockSpec((1, CHUNK), lambda i: (0, i)),
        ],
        out_specs=pl.BlockSpec((1, CHUNK), lambda i: (0, i)),
    )(field_rows, rows, lanes)


def add_kernel(values_ref, rows_ref, lanes_ref, out_ref):
    field_rows, lanes = out_ref.shape
    chunk = rows_ref.shape[1]

    @pl.when(pl.program_id(0) == 0)
    def _():
        out_ref[...] = jnp.zeros_like(out_ref)

    chosen = lax.broadcasted_iota(jnp.int32, (lanes, chunk), 0) == lanes_ref[...]
    placed = jnp.where(chosen, values_ref[...], 0.0)
    hot = (
        lax.broadcasted_iota(jnp.int32, (field_rows, chunk), 0) == rows_ref[...]
    ).astype(jnp.bfloat16)
    total = None
    for part in split_three(placed):
        term = lax.dot_general(
            hot, part, (((1,), (1,)), ((), ())), preferred_element_type=jnp.float32
        )
        total = term if total is None else total + term
    out_ref[...] += total


def add_cells(values, rows, lanes, field_rows, lane_count):
    count = rows.shape[1]
    return pl.pallas_call(
        add_kernel,
        out_shape=jax.ShapeDtypeStruct((field_rows, lane_count), jnp.float32),
        grid=(count // CHUNK,),
        in_specs=[
            pl.BlockSpec((1, CHUNK), lambda i: (0, i)),
            pl.BlockSpec((1, CHUNK), lambda i: (0, i)),
            pl.BlockSpec((1, CHUNK), lambda i: (0, i)),
        ],
        out_specs=pl.BlockSpec((field_rows, lane_count), lambda i: (0, 0)),
        compiler_params=pltpu.CompilerParams(dimension_semantics=("arbitrary",)),
    )(values, rows, lanes)


def exchange(values, partial):
    rows = values.shape[0]
    packed = jnp.concatenate(
        [values, jnp.broadcast_to(partial.astype(values.dtype), (rows, 1))], axis=1
    )
    arrived = lax.all_to_all(packed, ("gx", "gy"), split_axis=0, concat_axis=0, tiled=True)
    return arrived[:, :-1], jnp.sum(arrived[:, -1])


def on_device(rate_x, rate_y, land_mask, obs_cell, obs_count, innovation, obs_weight):
    ocean = land_mask.astype(jnp.float32)
    field_shape = (TR,) + rate_x.shape
    plan_along_x = make_plan(rate_x, 2, "gx", True)
    plan_along_y = make_plan(rate_y, 3, "gy", False)

    def along_x(state_field):
        return line_operator(state_field, plan_along_x)

    def along_y(state_field):
        return line_operator(state_field, plan_along_y)

    def spread(vector):
        return ocean * along_y(along_x(ocean * vector))

    def gather_back(vector):
        return ocean * along_x(along_y(ocean * vector))

    cell_index = obs_cell[0]
    occupied = (
        lax.broadcasted_iota(jnp.int32, cell_index.shape, 1) < obs_count[0][:, None]
    ).astype(jnp.float32)
    blocks = obs_weight[0]

    def weigh_obs(values):
        packed = (occupied * values).reshape(blocks.shape[0], blocks.shape[1])
        mixed = jnp.einsum("nij,nj->ni", blocks, packed, precision=lax.Precision.HIGHEST)
        return occupied * mixed.reshape(occupied.shape)

    lane_count = field_shape[-1]
    field_rows = TR * rate_x.size // lane_count
    flat_index = cell_index.reshape(1, -1)
    row_of = flat_index // lane_count
    lane_of = flat_index % lane_count

    def deposit_local(arrived):
        cells = add_cells(arrived.reshape(1, -1), row_of, lane_of, field_rows, lane_count)
        return cells.reshape(field_shape)

    def observe(vector):
        picked = pick_cells(vector.reshape(field_rows, lane_count), row_of, lane_of)
        return picked.reshape(cell_index.shape)

    weighted = weigh_obs(innovation[0])
    arrived = lax.all_to_all(weighted, ("gx", "gy"), split_axis=0, concat_axis=0, tiled=True)
    right_side = gather_back(deposit_local(arrived))
    solution = jnp.zeros_like(right_side)
    residual = right_side
    direction = right_side
    norm_now = None
    previous_seen = None
    for iteration in range(ITERS):
        seen, norm_next = exchange(observe(spread(residual)), jnp.sum(residual * residual))
        if iteration == 0:
            direction = residual
        else:
            ratio = norm_next / norm_now
            seen = seen + ratio * previous_seen
            direction = residual + ratio * direction
        norm_now = norm_next
        mixed = weigh_obs(seen)
        returned, curvature = exchange(
            mixed, jnp.sum(direction * direction) + jnp.sum(seen * mixed)
        )
        hessian_dir = direction + gather_back(deposit_local(returned))
        step_length = norm_now / curvature
        solution = solution + step_length * direction
        residual = residual - step_length * hessian_dir
        previous_seen = seen
    return (solution, residual)


def solution(mesh):
    placed = (
        P(None, "gx", "gy"),
        P(None, "gx", "gy"),
        P("gx", "gy"),
        P(("gx", "gy"), None, None),
        P(("gx", "gy"), None),
        P(("gx", "gy"), None, None),
        P(("gx", "gy"), None, None, None),
    )
    return jax.shard_map(
        on_device,
        mesh=mesh,
        in_specs=placed,
        out_specs=(P(None, None, "gx", "gy"), P(None, None, "gx", "gy")),
        check_vma=False,
    )
```

```python
import jax
import jax.numpy as jnp
from jax import lax
from jax.sharding import PartitionSpec as P

TR = 2
ITERS = 2


def shift_along(values, distance, line_axis, reverse, filler):
    length = values.shape[line_axis]
    edge_shape = list(values.shape)
    edge_shape[line_axis] = distance
    edge = jnp.full(tuple(edge_shape), filler, values.dtype)
    if reverse:
        return jnp.concatenate(
            [lax.slice_in_dim(values, distance, length, axis=line_axis), edge], axis=line_axis
        )
    return jnp.concatenate(
        [edge, lax.slice_in_dim(values, 0, length - distance, axis=line_axis)], axis=line_axis
    )


def factor_levels(retention, line_axis, reverse):
    length = retention.shape[line_axis]
    stored = []
    factor = retention
    distance = 1
    while distance < length:
        stored.append(factor)
        factor = factor * shift_along(factor, distance, line_axis, reverse, 1.0)
        distance = distance * 2
    return (stored, factor)


def scan_offsets(stored, forcing, line_axis, reverse):
    distance = 1
    for level_factor in stored:
        forcing = forcing + level_factor * shift_along(forcing, distance, line_axis, reverse, 0.0)
        distance = distance * 2
    return forcing


def make_plan(decay_rate, line_axis, axis_name, periodic):
    retention = jnp.exp(-decay_rate)[None]
    one_minus = -jnp.expm1(-decay_rate)
    scaling = jnp.sqrt(one_minus * (1.0 + jnp.exp(-decay_rate)))
    weight = jnp.sqrt(jnp.sqrt(one_minus))
    length = retention.shape[line_axis]
    forward_stored, prefix = factor_levels(retention, line_axis, False)
    backward_stored, suffix = factor_levels(retention, line_axis, True)
    back_of_prefix = scan_offsets(backward_stored, retention * prefix, line_axis, True)
    totals = jnp.stack(
        [
            lax.index_in_dim(prefix, length - 1, line_axis, keepdims=False),
            lax.index_in_dim(suffix, 0, line_axis, keepdims=False),
            lax.index_in_dim(back_of_prefix, 0, line_axis, keepdims=False),
        ]
    )
    return dict(
        retention=retention,
        gain=scaling * weight,
        gain_out=weight * scaling,
        forward_stored=forward_stored,
        backward_stored=backward_stored,
        prefix=prefix,
        suffix=suffix,
        back_of_prefix=back_of_prefix,
        rate_totals=lax.all_gather(totals, axis_name),
        axis_name=axis_name,
        periodic=periodic,
        line_axis=line_axis,
    )


def carries(got, rate_totals, periodic, axis_name):
    count = got.shape[0]
    offsets = [got[k, 0] for k in range(count)]
    back_parts = [got[k, 1] for k in range(count)]
    factors = [rate_totals[k, 0] for k in range(count)]
    back_factors = [rate_totals[k, 1] for k in range(count)]
    back_gains = [rate_totals[k, 2] for k in range(count)]
    if periodic:
        total = offsets[0]
        product = factors[0]
        for k in range(1, count):
            total = factors[k] * total + offsets[k]
            product = product * factors[k]
        first = total / (1.0 - product)
    else:
        first = jnp.zeros_like(offsets[0])
    place = lax.axis_index(axis_name)
    entering = [first]
    mine_in = first
    for k in range(count - 1):
        entering.append(offsets[k] + factors[k] * entering[k])
        mine_in = jnp.where(place > k, entering[k + 1], mine_in)
    back_totals = [back_parts[k] + entering[k] * back_gains[k] for k in range(count)]
    if periodic:
        total = back_totals[count - 1]
        product = back_factors[count - 1]
        for k in range(count - 2, -1, -1):
            total = back_totals[k] + back_factors[k] * total
            product = product * back_factors[k]
        leaving = total / (1.0 - product)
    else:
        leaving = jnp.zeros_like(offsets[0])
    mine_out = leaving
    for k in range(count - 2, -1, -1):
        leaving = back_totals[k + 1] + back_factors[k + 1] * leaving
        mine_out = jnp.where(place <= k, leaving, mine_out)
    return mine_in, mine_out


def line_operator(state_field, plan):
    line_axis = plan["line_axis"]
    length = state_field.shape[line_axis]
    offset = scan_offsets(plan["forward_stored"], plan["gain"] * state_field, line_axis, False)
    back_offset = scan_offsets(
        plan["backward_stored"], plan["retention"] * offset, line_axis, True
    )
    mine = jnp.stack(
        [
            lax.index_in_dim(offset, length - 1, line_axis, keepdims=False),
            lax.index_in_dim(back_offset, 0, line_axis, keepdims=False),
        ]
    )
    got = lax.all_gather(mine, plan["axis_name"])
    entering, leaving = carries(got, plan["rate_totals"], plan["periodic"], plan["axis_name"])
    entering = jnp.expand_dims(entering, line_axis)
    leaving = jnp.expand_dims(leaving, line_axis)
    forward = offset + plan["prefix"] * entering
    back_offset = back_offset + entering * plan["back_of_prefix"]
    next_factor = shift_along(plan["suffix"], 1, line_axis, True, 1.0)
    next_offset = shift_along(back_offset, 1, line_axis, True, 0.0)
    return plan["gain_out"] * (forward + next_offset + next_factor * leaving)


def exchange(values, partial):
    rows = values.shape[0]
    packed = jnp.concatenate(
        [values, jnp.broadcast_to(partial.astype(values.dtype), (rows, 1))], axis=1
    )
    arrived = lax.all_to_all(packed, ("gx", "gy"), split_axis=0, concat_axis=0, tiled=True)
    return arrived[:, :-1], jnp.sum(arrived[:, -1])


def on_device(rate_x, rate_y, land_mask, obs_cell, obs_count, innovation, obs_weight):
    ocean = land_mask.astype(jnp.float32)
    field_shape = (TR,) + rate_x.shape
    plan_along_x = make_plan(rate_x, 2, "gx", True)
    plan_along_y = make_plan(rate_y, 3, "gy", False)

    def along_x(state_field):
        return line_operator(state_field, plan_along_x)

    def along_y(state_field):
        return line_operator(state_field, plan_along_y)

    def spread(vector):
        return ocean * along_y(along_x(ocean * vector))

    def gather_back(vector):
        return ocean * along_x(along_y(ocean * vector))

    cell_index = obs_cell[0]
    occupied = (
        lax.broadcasted_iota(jnp.int32, cell_index.shape, 1) < obs_count[0][:, None]
    ).astype(jnp.float32)
    blocks = obs_weight[0]

    def weigh_obs(values):
        packed = (occupied * values).reshape(blocks.shape[0], blocks.shape[1])
        mixed = jnp.einsum("nij,nj->ni", blocks, packed, precision=lax.Precision.HIGHEST)
        return occupied * mixed.reshape(occupied.shape)

    def deposit_local(arrived):
        flat_cells = (
            jnp.zeros((TR * rate_x.size,), jnp.float32)
            .at[cell_index.reshape(-1)]
            .add(arrived.reshape(-1))
        )
        return flat_cells.reshape(field_shape)

    def observe(vector):
        return jnp.take(vector.reshape(-1), cell_index.reshape(-1), axis=0).reshape(
            cell_index.shape
        )

    weighted = weigh_obs(innovation[0])
    arrived = lax.all_to_all(weighted, ("gx", "gy"), split_axis=0, concat_axis=0, tiled=True)
    right_side = gather_back(deposit_local(arrived))
    solution = jnp.zeros_like(right_side)
    residual = right_side
    direction = right_side
    norm_now = None
    previous_seen = None
    for iteration in range(ITERS):
        seen, norm_next = exchange(observe(spread(residual)), jnp.sum(residual * residual))
        if iteration == 0:
            direction = residual
        else:
            ratio = norm_next / norm_now
            seen = seen + ratio * previous_seen
            direction = residual + ratio * direction
        norm_now = norm_next
        mixed = weigh_obs(seen)
        returned, curvature = exchange(
            mixed, jnp.sum(direction * direction) + jnp.sum(seen * mixed)
        )
        hessian_dir = direction + gather_back(deposit_local(returned))
        step_length = norm_now / curvature
        solution = solution + step_length * direction
        residual = residual - step_length * hessian_dir
        previous_seen = seen
    return (solution, residual)


def solution(mesh):
    placed = (
        P(None, "gx", "gy"),
        P(None, "gx", "gy"),
        P("gx", "gy"),
        P(("gx", "gy"), None, None),
        P(("gx", "gy"), None),
        P(("gx", "gy"), None, None),
        P(("gx", "gy"), None, None, None),
    )
    return jax.shard_map(
        on_device,
        mesh=mesh,
        in_specs=placed,
        out_specs=(P(None, None, "gx", "gy"), P(None, None, "gx", "gy")),
        check_vma=False,
    )
```

```python
import jax
import jax.numpy as jnp
from jax import lax
from jax.sharding import PartitionSpec as P
from jax.experimental import pallas as pl
from jax.experimental.pallas import tpu as pltpu

TR = 2
ITERS = 2


def shift_along(values, distance, line_axis, reverse, filler):
    length = values.shape[line_axis]
    edge_shape = list(values.shape)
    edge_shape[line_axis] = distance
    edge = jnp.full(tuple(edge_shape), filler, values.dtype)
    if reverse:
        return jnp.concatenate(
            [lax.slice_in_dim(values, distance, length, axis=line_axis), edge], axis=line_axis
        )
    return jnp.concatenate(
        [edge, lax.slice_in_dim(values, 0, length - distance, axis=line_axis)], axis=line_axis
    )


def factor_levels(retention, line_axis, reverse):
    length = retention.shape[line_axis]
    stored = []
    factor = retention
    distance = 1
    while distance < length:
        stored.append(factor)
        factor = factor * shift_along(factor, distance, line_axis, reverse, 1.0)
        distance = distance * 2
    return (stored, factor)


def scan_offsets(stored, forcing, line_axis, reverse):
    distance = 1
    for level_factor in stored:
        forcing = forcing + level_factor * shift_along(forcing, distance, line_axis, reverse, 0.0)
        distance = distance * 2
    return forcing


def make_plan(decay_rate, line_axis, axis_name, periodic):
    retention = jnp.exp(-decay_rate)[None]
    one_minus = -jnp.expm1(-decay_rate)
    scaling = jnp.sqrt(one_minus * (1.0 + jnp.exp(-decay_rate)))
    weight = jnp.sqrt(jnp.sqrt(one_minus))
    length = retention.shape[line_axis]
    forward_stored, prefix = factor_levels(retention, line_axis, False)
    backward_stored, suffix = factor_levels(retention, line_axis, True)
    back_of_prefix = scan_offsets(backward_stored, retention * prefix, line_axis, True)
    totals = jnp.stack(
        [
            lax.index_in_dim(prefix, length - 1, line_axis, keepdims=False),
            lax.index_in_dim(suffix, 0, line_axis, keepdims=False),
            lax.index_in_dim(back_of_prefix, 0, line_axis, keepdims=False),
        ]
    )
    return dict(
        retention=retention,
        gain=scaling * weight,
        gain_out=weight * scaling,
        forward_stored=forward_stored,
        backward_stored=backward_stored,
        prefix=prefix,
        suffix=suffix,
        back_of_prefix=back_of_prefix,
        rate_totals=lax.all_gather(totals, axis_name),
        axis_name=axis_name,
        periodic=periodic,
        line_axis=line_axis,
    )


def carries(got, rate_totals, periodic, axis_name):
    count = got.shape[0]
    offsets = [got[k, 0] for k in range(count)]
    back_parts = [got[k, 1] for k in range(count)]
    factors = [rate_totals[k, 0] for k in range(count)]
    back_factors = [rate_totals[k, 1] for k in range(count)]
    back_gains = [rate_totals[k, 2] for k in range(count)]
    if periodic:
        total = offsets[0]
        product = factors[0]
        for k in range(1, count):
            total = factors[k] * total + offsets[k]
            product = product * factors[k]
        first = total / (1.0 - product)
    else:
        first = jnp.zeros_like(offsets[0])
    entering = [first]
    for k in range(count - 1):
        entering.append(offsets[k] + factors[k] * entering[k])
    back_totals = [back_parts[k] + entering[k] * back_gains[k] for k in range(count)]
    if periodic:
        total = back_totals[count - 1]
        product = back_factors[count - 1]
        for k in range(count - 2, -1, -1):
            total = back_totals[k] + back_factors[k] * total
            product = product * back_factors[k]
        last = total / (1.0 - product)
    else:
        last = jnp.zeros_like(offsets[0])
    leaving = [None] * count
    leaving[count - 1] = last
    for k in range(count - 2, -1, -1):
        leaving[k] = back_totals[k + 1] + back_factors[k + 1] * leaving[k + 1]
    place = lax.axis_index(axis_name)
    mine_in = lax.dynamic_index_in_dim(jnp.stack(entering), place, 0, False)
    mine_out = lax.dynamic_index_in_dim(jnp.stack(leaving), place, 0, False)
    return mine_in, mine_out


def line_operator(state_field, plan):
    line_axis = plan["line_axis"]
    length = state_field.shape[line_axis]
    offset = scan_offsets(plan["forward_stored"], plan["gain"] * state_field, line_axis, False)
    back_offset = scan_offsets(
        plan["backward_stored"], plan["retention"] * offset, line_axis, True
    )
    mine = jnp.stack(
        [
            lax.index_in_dim(offset, length - 1, line_axis, keepdims=False),
            lax.index_in_dim(back_offset, 0, line_axis, keepdims=False),
        ]
    )
    got = lax.all_gather(mine, plan["axis_name"])
    entering, leaving = carries(got, plan["rate_totals"], plan["periodic"], plan["axis_name"])
    entering = jnp.expand_dims(entering, line_axis)
    leaving = jnp.expand_dims(leaving, line_axis)
    forward = offset + plan["prefix"] * entering
    back_offset = back_offset + entering * plan["back_of_prefix"]
    next_factor = shift_along(plan["suffix"], 1, line_axis, True, 1.0)
    next_offset = shift_along(back_offset, 1, line_axis, True, 0.0)
    return plan["gain_out"] * (forward + next_offset + next_factor * leaving)


CHUNK = 512


def split_three(values):
    high = values.astype(jnp.bfloat16)
    rest = values - high.astype(jnp.float32)
    middle = rest.astype(jnp.bfloat16)
    low = (rest - middle.astype(jnp.float32)).astype(jnp.bfloat16)
    return high, middle, low


def pick_kernel(field_ref, rows_ref, lanes_ref, out_ref):
    field_rows, lanes = field_ref.shape
    chunk = rows_ref.shape[1]
    parts = split_three(field_ref[...].T)
    hot = (
        lax.broadcasted_iota(jnp.int32, (field_rows, chunk), 0) == rows_ref[...]
    ).astype(jnp.bfloat16)
    picked = None
    for part in parts:
        term = jnp.dot(part, hot, preferred_element_type=jnp.float32)
        picked = term if picked is None else picked + term
    chosen = lax.broadcasted_iota(jnp.int32, (lanes, chunk), 0) == lanes_ref[...]
    out_ref[...] = jnp.sum(jnp.where(chosen, picked, 0.0), axis=0, keepdims=True)


def pick_cells(field_rows, rows, lanes):
    count = rows.shape[1]
    return pl.pallas_call(
        pick_kernel,
        out_shape=jax.ShapeDtypeStruct((1, count), jnp.float32),
        grid=(count // CHUNK,),
        in_specs=[
            pl.BlockSpec(field_rows.shape, lambda i: (0, 0)),
            pl.BlockSpec((1, CHUNK), lambda i: (0, i)),
            pl.BlockSpec((1, CHUNK), lambda i: (0, i)),
        ],
        out_specs=pl.BlockSpec((1, CHUNK), lambda i: (0, i)),
    )(field_rows, rows, lanes)


def add_kernel(values_ref, rows_ref, lanes_ref, out_ref):
    field_rows, lanes = out_ref.shape
    chunk = rows_ref.shape[1]

    @pl.when(pl.program_id(0) == 0)
    def _():
        out_ref[...] = jnp.zeros_like(out_ref)

    chosen = lax.broadcasted_iota(jnp.int32, (lanes, chunk), 0) == lanes_ref[...]
    placed = jnp.where(chosen, values_ref[...], 0.0)
    hot = (
        lax.broadcasted_iota(jnp.int32, (field_rows, chunk), 0) == rows_ref[...]
    ).astype(jnp.bfloat16)
    total = None
    for part in split_three(placed):
        term = lax.dot_general(
            hot, part, (((1,), (1,)), ((), ())), preferred_element_type=jnp.float32
        )
        total = term if total is None else total + term
    out_ref[...] += total


def add_cells(values, rows, lanes, field_rows, lane_count):
    count = rows.shape[1]
    return pl.pallas_call(
        add_kernel,
        out_shape=jax.ShapeDtypeStruct((field_rows, lane_count), jnp.float32),
        grid=(count // CHUNK,),
        in_specs=[
            pl.BlockSpec((1, CHUNK), lambda i: (0, i)),
            pl.BlockSpec((1, CHUNK), lambda i: (0, i)),
            pl.BlockSpec((1, CHUNK), lambda i: (0, i)),
        ],
        out_specs=pl.BlockSpec((field_rows, lane_count), lambda i: (0, 0)),
        compiler_params=pltpu.CompilerParams(dimension_semantics=("arbitrary",)),
    )(values, rows, lanes)


def exchange(values, partial):
    rows = values.shape[0]
    packed = jnp.concatenate(
        [values, jnp.broadcast_to(partial.astype(values.dtype), (rows, 1))], axis=1
    )
    arrived = lax.all_to_all(packed, ("gx", "gy"), split_axis=0, concat_axis=0, tiled=True)
    return arrived[:, :-1], jnp.sum(arrived[:, -1])


def on_device(rate_x, rate_y, land_mask, obs_cell, obs_count, innovation, obs_weight):
    ocean = land_mask.astype(jnp.float32)
    field_shape = (TR,) + rate_x.shape
    plan_along_x = make_plan(rate_x, 2, "gx", True)
    plan_along_y = make_plan(rate_y, 3, "gy", False)

    def along_x(state_field):
        return line_operator(state_field, plan_along_x)

    def along_y(state_field):
        return line_operator(state_field, plan_along_y)

    def spread(vector):
        return ocean * along_y(along_x(ocean * vector))

    def gather_back(vector):
        return ocean * along_x(along_y(ocean * vector))

    cell_index = obs_cell[0]
    occupied = (
        lax.broadcasted_iota(jnp.int32, cell_index.shape, 1) < obs_count[0][:, None]
    ).astype(jnp.float32)
    blocks = obs_weight[0]

    def weigh_obs(values):
        packed = (occupied * values).reshape(blocks.shape[0], blocks.shape[1])
        mixed = jnp.einsum("nij,nj->ni", blocks, packed, precision=lax.Precision.HIGHEST)
        return occupied * mixed.reshape(occupied.shape)

    lane_count = field_shape[-1]
    field_rows = TR * rate_x.size // lane_count
    flat_index = cell_index.reshape(1, -1)
    row_of = flat_index // lane_count
    lane_of = flat_index % lane_count

    def deposit_local(arrived):
        flat_cells = (
            jnp.zeros((TR * rate_x.size,), jnp.float32)
            .at[cell_index.reshape(-1)]
            .add(arrived.reshape(-1))
        )
        return flat_cells.reshape(field_shape)

    def observe(vector):
        picked = pick_cells(vector.reshape(field_rows, lane_count), row_of, lane_of)
        return picked.reshape(cell_index.shape)

    weighted = weigh_obs(innovation[0])
    arrived = lax.all_to_all(weighted, ("gx", "gy"), split_axis=0, concat_axis=0, tiled=True)
    right_side = gather_back(deposit_local(arrived))
    solution = jnp.zeros_like(right_side)
    residual = right_side
    direction = right_side
    norm_now = None
    previous_seen = None
    for iteration in range(ITERS):
        seen, norm_next = exchange(observe(spread(residual)), jnp.sum(residual * residual))
        if iteration == 0:
            direction = residual
        else:
            ratio = norm_next / norm_now
            seen = seen + ratio * previous_seen
            direction = residual + ratio * direction
        norm_now = norm_next
        mixed = weigh_obs(seen)
        returned, curvature = exchange(
            mixed, jnp.sum(direction * direction) + jnp.sum(seen * mixed)
        )
        hessian_dir = direction + gather_back(deposit_local(returned))
        step_length = norm_now / curvature
        solution = solution + step_length * direction
        residual = residual - step_length * hessian_dir
        previous_seen = seen
    return (solution, residual)


def solution(mesh):
    placed = (
        P(None, "gx", "gy"),
        P(None, "gx", "gy"),
        P("gx", "gy"),
        P(("gx", "gy"), None, None),
        P(("gx", "gy"), None),
        P(("gx", "gy"), None, None),
        P(("gx", "gy"), None, None, None),
    )
    return jax.shard_map(
        on_device,
        mesh=mesh,
        in_specs=placed,
        out_specs=(P(None, None, "gx", "gy"), P(None, None, "gx", "gy")),
        check_vma=False,
    )
```

```python
import jax
import jax.numpy as jnp
from jax import lax
from jax.sharding import PartitionSpec as P
from jax.experimental import pallas as pl
from jax.experimental.pallas import tpu as pltpu

TR = 2
ITERS = 2


def shift_along(values, distance, line_axis, reverse, filler):
    length = values.shape[line_axis]
    edge_shape = list(values.shape)
    edge_shape[line_axis] = distance
    edge = jnp.full(tuple(edge_shape), filler, values.dtype)
    if reverse:
        return jnp.concatenate(
            [lax.slice_in_dim(values, distance, length, axis=line_axis), edge], axis=line_axis
        )
    return jnp.concatenate(
        [edge, lax.slice_in_dim(values, 0, length - distance, axis=line_axis)], axis=line_axis
    )


def factor_levels(retention, line_axis, reverse):
    length = retention.shape[line_axis]
    stored = []
    factor = retention
    distance = 1
    while distance < length:
        stored.append(factor)
        factor = factor * shift_along(factor, distance, line_axis, reverse, 1.0)
        distance = distance * 2
    return (stored, factor)


def scan_offsets(stored, forcing, line_axis, reverse):
    distance = 1
    for level_factor in stored:
        forcing = forcing + level_factor * shift_along(forcing, distance, line_axis, reverse, 0.0)
        distance = distance * 2
    return forcing


def make_plan(decay_rate, line_axis, axis_name, periodic):
    retention = jnp.exp(-decay_rate)[None]
    one_minus = -jnp.expm1(-decay_rate)
    scaling = jnp.sqrt(one_minus * (1.0 + jnp.exp(-decay_rate)))
    weight = jnp.sqrt(jnp.sqrt(one_minus))
    length = retention.shape[line_axis]
    forward_stored, prefix = factor_levels(retention, line_axis, False)
    backward_stored, suffix = factor_levels(retention, line_axis, True)
    back_of_prefix = scan_offsets(backward_stored, retention * prefix, line_axis, True)
    totals = jnp.stack(
        [
            lax.index_in_dim(prefix, length - 1, line_axis, keepdims=False),
            lax.index_in_dim(suffix, 0, line_axis, keepdims=False),
            lax.index_in_dim(back_of_prefix, 0, line_axis, keepdims=False),
        ]
    )
    rate_totals = lax.all_gather(totals, axis_name)
    count = rate_totals.shape[0]
    basis = jnp.arange(2 * count, dtype=jnp.int32).reshape(2 * count, 1, 1, 1)
    unit_in, unit_out = carries(
        [(basis == k).astype(jnp.float32) for k in range(count)],
        [(basis == count + k).astype(jnp.float32) for k in range(count)],
        rate_totals,
        periodic,
        axis_name,
    )
    return dict(
        entering_weights=unit_in[:count],
        leaving_weights=unit_out[:count],
        leaving_back_weights=unit_out[count:],
        retention=retention,
        gain=scaling * weight,
        gain_out=weight * scaling,
        forward_stored=forward_stored,
        backward_stored=backward_stored,
        prefix=prefix,
        suffix=suffix,
        back_of_prefix=back_of_prefix,
        axis_name=axis_name,
        periodic=periodic,
        line_axis=line_axis,
    )


def carries(offsets, back_parts, rate_totals, periodic, axis_name):
    count = len(offsets)
    factors = [rate_totals[k, 0] for k in range(count)]
    back_factors = [rate_totals[k, 1] for k in range(count)]
    back_gains = [rate_totals[k, 2] for k in range(count)]
    if periodic:
        total = offsets[0]
        product = factors[0]
        for k in range(1, count):
            total = factors[k] * total + offsets[k]
            product = product * factors[k]
        first = total / (1.0 - product)
    else:
        first = jnp.zeros_like(offsets[0] * factors[0])
    entering = [first]
    for k in range(count - 1):
        entering.append(offsets[k] + factors[k] * entering[k])
    back_totals = [back_parts[k] + entering[k] * back_gains[k] for k in range(count)]
    if periodic:
        total = back_totals[count - 1]
        product = back_factors[count - 1]
        for k in range(count - 2, -1, -1):
            total = back_totals[k] + back_factors[k] * total
            product = product * back_factors[k]
        last = total / (1.0 - product)
    else:
        last = jnp.zeros_like(offsets[0] * factors[0])
    leaving = [None] * count
    leaving[count - 1] = last
    for k in range(count - 2, -1, -1):
        leaving[k] = back_totals[k + 1] + back_factors[k + 1] * leaving[k + 1]
    place = lax.axis_index(axis_name)
    mine_in = lax.dynamic_index_in_dim(jnp.stack(entering), place, 0, False)
    mine_out = lax.dynamic_index_in_dim(jnp.stack(leaving), place, 0, False)
    return mine_in, mine_out


def line_operator(state_field, plan):
    line_axis = plan["line_axis"]
    length = state_field.shape[line_axis]
    offset = scan_offsets(plan["forward_stored"], plan["gain"] * state_field, line_axis, False)
    back_offset = scan_offsets(
        plan["backward_stored"], plan["retention"] * offset, line_axis, True
    )
    mine = jnp.stack(
        [
            lax.index_in_dim(offset, length - 1, line_axis, keepdims=False),
            lax.index_in_dim(back_offset, 0, line_axis, keepdims=False),
        ]
    )
    got = lax.all_gather(mine, plan["axis_name"])
    entering = jnp.sum(plan["entering_weights"] * got[:, 0], axis=0)
    leaving = jnp.sum(
        plan["leaving_weights"] * got[:, 0] + plan["leaving_back_weights"] * got[:, 1], axis=0
    )
    entering = jnp.expand_dims(entering, line_axis)
    leaving = jnp.expand_dims(leaving, line_axis)
    forward = offset + plan["prefix"] * entering
    back_offset = back_offset + entering * plan["back_of_prefix"]
    next_factor = shift_along(plan["suffix"], 1, line_axis, True, 1.0)
    next_offset = shift_along(back_offset, 1, line_axis, True, 0.0)
    return plan["gain_out"] * (forward + next_offset + next_factor * leaving)


CHUNK = 512


def split_three(values):
    high = values.astype(jnp.bfloat16)
    rest = values - high.astype(jnp.float32)
    middle = rest.astype(jnp.bfloat16)
    low = (rest - middle.astype(jnp.float32)).astype(jnp.bfloat16)
    return high, middle, low


def pick_kernel(field_ref, rows_ref, lanes_ref, out_ref):
    field_rows, lanes = field_ref.shape
    chunk = rows_ref.shape[1]
    parts = split_three(field_ref[...].T)
    hot = (
        lax.broadcasted_iota(jnp.int32, (field_rows, chunk), 0) == rows_ref[...]
    ).astype(jnp.bfloat16)
    picked = None
    for part in parts:
        term = jnp.dot(part, hot, preferred_element_type=jnp.float32)
        picked = term if picked is None else picked + term
    chosen = lax.broadcasted_iota(jnp.int32, (lanes, chunk), 0) == lanes_ref[...]
    out_ref[...] = jnp.sum(jnp.where(chosen, picked, 0.0), axis=0, keepdims=True)


def pick_cells(field_rows, rows, lanes):
    count = rows.shape[1]
    return pl.pallas_call(
        pick_kernel,
        out_shape=jax.ShapeDtypeStruct((1, count), jnp.float32),
        grid=(count // CHUNK,),
        in_specs=[
            pl.BlockSpec(field_rows.shape, lambda i: (0, 0)),
            pl.BlockSpec((1, CHUNK), lambda i: (0, i)),
            pl.BlockSpec((1, CHUNK), lambda i: (0, i)),
        ],
        out_specs=pl.BlockSpec((1, CHUNK), lambda i: (0, i)),
    )(field_rows, rows, lanes)


def add_kernel(values_ref, rows_ref, lanes_ref, out_ref):
    field_rows, lanes = out_ref.shape
    chunk = rows_ref.shape[1]

    @pl.when(pl.program_id(0) == 0)
    def _():
        out_ref[...] = jnp.zeros_like(out_ref)

    chosen = lax.broadcasted_iota(jnp.int32, (lanes, chunk), 0) == lanes_ref[...]
    placed = jnp.where(chosen, values_ref[...], 0.0)
    hot = (
        lax.broadcasted_iota(jnp.int32, (field_rows, chunk), 0) == rows_ref[...]
    ).astype(jnp.bfloat16)
    total = None
    for part in split_three(placed):
        term = lax.dot_general(
            hot, part, (((1,), (1,)), ((), ())), preferred_element_type=jnp.float32
        )
        total = term if total is None else total + term
    out_ref[...] += total


def add_cells(values, rows, lanes, field_rows, lane_count):
    count = rows.shape[1]
    return pl.pallas_call(
        add_kernel,
        out_shape=jax.ShapeDtypeStruct((field_rows, lane_count), jnp.float32),
        grid=(count // CHUNK,),
        in_specs=[
            pl.BlockSpec((1, CHUNK), lambda i: (0, i)),
            pl.BlockSpec((1, CHUNK), lambda i: (0, i)),
            pl.BlockSpec((1, CHUNK), lambda i: (0, i)),
        ],
        out_specs=pl.BlockSpec((field_rows, lane_count), lambda i: (0, 0)),
        compiler_params=pltpu.CompilerParams(dimension_semantics=("arbitrary",)),
    )(values, rows, lanes)


def exchange(values, partial):
    rows = values.shape[0]
    packed = jnp.concatenate(
        [values, jnp.broadcast_to(partial.astype(values.dtype), (rows, 1))], axis=1
    )
    arrived = lax.all_to_all(packed, ("gx", "gy"), split_axis=0, concat_axis=0, tiled=True)
    return arrived[:, :-1], jnp.sum(arrived[:, -1])


def on_device(rate_x, rate_y, land_mask, obs_cell, obs_count, innovation, obs_weight):
    ocean = land_mask.astype(jnp.float32)
    field_shape = (TR,) + rate_x.shape
    plan_along_x = make_plan(rate_x, 2, "gx", True)
    plan_along_y = make_plan(rate_y, 3, "gy", False)

    def along_x(state_field):
        return line_operator(state_field, plan_along_x)

    def along_y(state_field):
        return line_operator(state_field, plan_along_y)

    def spread(vector):
        return ocean * along_y(along_x(ocean * vector))

    def gather_back(vector):
        return ocean * along_x(along_y(ocean * vector))

    cell_index = obs_cell[0]
    occupied = (
        lax.broadcasted_iota(jnp.int32, cell_index.shape, 1) < obs_count[0][:, None]
    ).astype(jnp.float32)
    blocks = obs_weight[0]

    def weigh_obs(values):
        packed = (occupied * values).reshape(blocks.shape[0], blocks.shape[1])
        mixed = jnp.einsum("nij,nj->ni", blocks, packed, precision=lax.Precision.HIGHEST)
        return occupied * mixed.reshape(occupied.shape)

    lane_count = field_shape[-1]
    field_rows = TR * rate_x.size // lane_count
    flat_index = cell_index.reshape(1, -1)
    row_of = flat_index // lane_count
    lane_of = flat_index % lane_count

    def deposit_local(arrived):
        flat_cells = (
            jnp.zeros((TR * rate_x.size,), jnp.float32)
            .at[cell_index.reshape(-1)]
            .add(arrived.reshape(-1))
        )
        return flat_cells.reshape(field_shape)

    def observe(vector):
        picked = pick_cells(vector.reshape(field_rows, lane_count), row_of, lane_of)
        return picked.reshape(cell_index.shape)

    weighted = weigh_obs(innovation[0])
    arrived = lax.all_to_all(weighted, ("gx", "gy"), split_axis=0, concat_axis=0, tiled=True)
    right_side = gather_back(deposit_local(arrived))
    solution = jnp.zeros_like(right_side)
    residual = right_side
    direction = right_side
    norm_now = None
    previous_seen = None
    for iteration in range(ITERS):
        seen, norm_next = exchange(observe(spread(residual)), jnp.sum(residual * residual))
        if iteration == 0:
            direction = residual
        else:
            ratio = norm_next / norm_now
            seen = seen + ratio * previous_seen
            direction = residual + ratio * direction
        norm_now = norm_next
        mixed = weigh_obs(seen)
        returned, curvature = exchange(
            mixed, jnp.sum(direction * direction) + jnp.sum(seen * mixed)
        )
        hessian_dir = direction + gather_back(deposit_local(returned))
        step_length = norm_now / curvature
        solution = solution + step_length * direction
        residual = residual - step_length * hessian_dir
        previous_seen = seen
    return (solution, residual)


def solution(mesh):
    placed = (
        P(None, "gx", "gy"),
        P(None, "gx", "gy"),
        P("gx", "gy"),
        P(("gx", "gy"), None, None),
        P(("gx", "gy"), None),
        P(("gx", "gy"), None, None),
        P(("gx", "gy"), None, None, None),
    )
    return jax.shard_map(
        on_device,
        mesh=mesh,
        in_specs=placed,
        out_specs=(P(None, None, "gx", "gy"), P(None, None, "gx", "gy")),
        check_vma=False,
    )
```

```python
import jax
import jax.numpy as jnp
from jax import lax
from jax.sharding import PartitionSpec as P
from jax.experimental import pallas as pl
from jax.experimental.pallas import tpu as pltpu

TR = 2
ITERS = 2


def shift_along(values, distance, line_axis, reverse, filler):
    length = values.shape[line_axis]
    edge_shape = list(values.shape)
    edge_shape[line_axis] = distance
    edge = jnp.full(tuple(edge_shape), filler, values.dtype)
    if reverse:
        return jnp.concatenate(
            [lax.slice_in_dim(values, distance, length, axis=line_axis), edge], axis=line_axis
        )
    return jnp.concatenate(
        [edge, lax.slice_in_dim(values, 0, length - distance, axis=line_axis)], axis=line_axis
    )


def factor_levels(retention, line_axis, reverse):
    length = retention.shape[line_axis]
    stored = []
    factor = retention
    distance = 1
    while distance < length:
        stored.append(factor)
        factor = factor * shift_along(factor, distance, line_axis, reverse, 1.0)
        distance = distance * 2
    return (stored, factor)


def scan_offsets(stored, forcing, line_axis, reverse):
    distance = 1
    for level_factor in stored:
        forcing = forcing + level_factor * shift_along(forcing, distance, line_axis, reverse, 0.0)
        distance = distance * 2
    return forcing


def make_plan(decay_rate, line_axis, axis_name, periodic):
    retention = jnp.exp(-decay_rate)[None]
    one_minus = -jnp.expm1(-decay_rate)
    scaling = jnp.sqrt(one_minus * (1.0 + jnp.exp(-decay_rate)))
    weight = jnp.sqrt(jnp.sqrt(one_minus))
    length = retention.shape[line_axis]
    forward_stored, prefix = factor_levels(retention, line_axis, False)
    backward_stored, suffix = factor_levels(retention, line_axis, True)
    back_of_prefix = scan_offsets(backward_stored, retention * prefix, line_axis, True)
    totals = jnp.stack(
        [
            lax.index_in_dim(prefix, length - 1, line_axis, keepdims=False),
            lax.index_in_dim(suffix, 0, line_axis, keepdims=False),
            lax.index_in_dim(back_of_prefix, 0, line_axis, keepdims=False),
        ]
    )
    return dict(
        retention=retention,
        gain=scaling * weight,
        gain_out=weight * scaling,
        forward_stored=forward_stored,
        backward_stored=backward_stored,
        prefix=prefix,
        suffix=suffix,
        back_of_prefix=back_of_prefix,
        rate_totals=lax.all_gather(totals, axis_name) if periodic else None,
        totals=totals,
        axis_name=axis_name,
        periodic=periodic,
        line_axis=line_axis,
    )


def carries(got, rate_totals, periodic, axis_name):
    count = got.shape[0]
    offsets = [got[k, 0] for k in range(count)]
    back_parts = [got[k, 1] for k in range(count)]
    factors = [rate_totals[k, 0] for k in range(count)]
    back_factors = [rate_totals[k, 1] for k in range(count)]
    back_gains = [rate_totals[k, 2] for k in range(count)]
    if periodic:
        total = offsets[0]
        product = factors[0]
        for k in range(1, count):
            total = factors[k] * total + offsets[k]
            product = product * factors[k]
        first = total / (1.0 - product)
    else:
        first = jnp.zeros_like(offsets[0])
    entering = [first]
    for k in range(count - 1):
        entering.append(offsets[k] + factors[k] * entering[k])
    back_totals = [back_parts[k] + entering[k] * back_gains[k] for k in range(count)]
    if periodic:
        total = back_totals[count - 1]
        product = back_factors[count - 1]
        for k in range(count - 2, -1, -1):
            total = back_totals[k] + back_factors[k] * total
            product = product * back_factors[k]
        last = total / (1.0 - product)
    else:
        last = jnp.zeros_like(offsets[0])
    leaving = [None] * count
    leaving[count - 1] = last
    for k in range(count - 2, -1, -1):
        leaving[k] = back_totals[k + 1] + back_factors[k + 1] * leaving[k + 1]
    place = lax.axis_index(axis_name)
    mine_in = lax.dynamic_index_in_dim(jnp.stack(entering), place, 0, False)
    mine_out = lax.dynamic_index_in_dim(jnp.stack(leaving), place, 0, False)
    return mine_in, mine_out


def line_operator(state_field, plan):
    line_axis = plan["line_axis"]
    length = state_field.shape[line_axis]
    offset = scan_offsets(plan["forward_stored"], plan["gain"] * state_field, line_axis, False)
    back_offset = scan_offsets(
        plan["backward_stored"], plan["retention"] * offset, line_axis, True
    )
    mine = jnp.stack(
        [
            lax.index_in_dim(offset, length - 1, line_axis, keepdims=False),
            lax.index_in_dim(back_offset, 0, line_axis, keepdims=False),
        ]
    )
    if plan["rate_totals"] is None:
        rate_part = jnp.broadcast_to(plan["totals"], (3,) + mine.shape[1:])
        both = lax.all_gather(jnp.concatenate([mine, rate_part]), plan["axis_name"])
        got = both[:, :2]
        plan["rate_totals"] = both[:, 2:, :1]
    else:
        got = lax.all_gather(mine, plan["axis_name"])
    entering, leaving = carries(got, plan["rate_totals"], plan["periodic"], plan["axis_name"])
    entering = jnp.expand_dims(entering, line_axis)
    leaving = jnp.expand_dims(leaving, line_axis)
    forward = offset + plan["prefix"] * entering
    back_offset = back_offset + entering * plan["back_of_prefix"]
    next_factor = shift_along(plan["suffix"], 1, line_axis, True, 1.0)
    next_offset = shift_along(back_offset, 1, line_axis, True, 0.0)
    return plan["gain_out"] * (forward + next_offset + next_factor * leaving)


CHUNK = 512


def split_three(values):
    high = values.astype(jnp.bfloat16)
    rest = values - high.astype(jnp.float32)
    middle = rest.astype(jnp.bfloat16)
    low = (rest - middle.astype(jnp.float32)).astype(jnp.bfloat16)
    return high, middle, low


def pick_kernel(field_ref, rows_ref, lanes_ref, out_ref):
    field_rows, lanes = field_ref.shape
    chunk = rows_ref.shape[1]
    parts = split_three(field_ref[...].T)
    hot = (
        lax.broadcasted_iota(jnp.int32, (field_rows, chunk), 0) == rows_ref[...]
    ).astype(jnp.bfloat16)
    picked = None
    for part in parts:
        term = jnp.dot(part, hot, preferred_element_type=jnp.float32)
        picked = term if picked is None else picked + term
    chosen = lax.broadcasted_iota(jnp.int32, (lanes, chunk), 0) == lanes_ref[...]
    out_ref[...] = jnp.sum(jnp.where(chosen, picked, 0.0), axis=0, keepdims=True)


def pick_cells(field_rows, rows, lanes):
    count = rows.shape[1]
    return pl.pallas_call(
        pick_kernel,
        out_shape=jax.ShapeDtypeStruct((1, count), jnp.float32),
        grid=(count // CHUNK,),
        in_specs=[
            pl.BlockSpec(field_rows.shape, lambda i: (0, 0)),
            pl.BlockSpec((1, CHUNK), lambda i: (0, i)),
            pl.BlockSpec((1, CHUNK), lambda i: (0, i)),
        ],
        out_specs=pl.BlockSpec((1, CHUNK), lambda i: (0, i)),
    )(field_rows, rows, lanes)


def add_kernel(values_ref, rows_ref, lanes_ref, out_ref):
    field_rows, lanes = out_ref.shape
    chunk = rows_ref.shape[1]

    @pl.when(pl.program_id(0) == 0)
    def _():
        out_ref[...] = jnp.zeros_like(out_ref)

    chosen = lax.broadcasted_iota(jnp.int32, (lanes, chunk), 0) == lanes_ref[...]
    placed = jnp.where(chosen, values_ref[...], 0.0)
    hot = (
        lax.broadcasted_iota(jnp.int32, (field_rows, chunk), 0) == rows_ref[...]
    ).astype(jnp.bfloat16)
    total = None
    for part in split_three(placed):
        term = lax.dot_general(
            hot, part, (((1,), (1,)), ((), ())), preferred_element_type=jnp.float32
        )
        total = term if total is None else total + term
    out_ref[...] += total


def add_cells(values, rows, lanes, field_rows, lane_count):
    count = rows.shape[1]
    return pl.pallas_call(
        add_kernel,
        out_shape=jax.ShapeDtypeStruct((field_rows, lane_count), jnp.float32),
        grid=(count // CHUNK,),
        in_specs=[
            pl.BlockSpec((1, CHUNK), lambda i: (0, i)),
            pl.BlockSpec((1, CHUNK), lambda i: (0, i)),
            pl.BlockSpec((1, CHUNK), lambda i: (0, i)),
        ],
        out_specs=pl.BlockSpec((field_rows, lane_count), lambda i: (0, 0)),
        compiler_params=pltpu.CompilerParams(dimension_semantics=("arbitrary",)),
    )(values, rows, lanes)


def exchange(values, partial):
    rows = values.shape[0]
    packed = jnp.concatenate(
        [values, jnp.broadcast_to(partial.astype(values.dtype), (rows, 1))], axis=1
    )
    arrived = lax.all_to_all(packed, ("gx", "gy"), split_axis=0, concat_axis=0, tiled=True)
    return arrived[:, :-1], jnp.sum(arrived[:, -1])


def on_device(rate_x, rate_y, land_mask, obs_cell, obs_count, innovation, obs_weight):
    ocean = land_mask.astype(jnp.float32)
    field_shape = (TR,) + rate_x.shape
    plan_along_x = make_plan(rate_x, 2, "gx", True)
    plan_along_y = make_plan(rate_y, 3, "gy", False)

    def along_x(state_field):
        return line_operator(state_field, plan_along_x)

    def along_y(state_field):
        return line_operator(state_field, plan_along_y)

    def spread(vector):
        return ocean * along_y(along_x(ocean * vector))

    def gather_back(vector):
        return ocean * along_x(along_y(ocean * vector))

    cell_index = obs_cell[0]
    occupied = (
        lax.broadcasted_iota(jnp.int32, cell_index.shape, 1) < obs_count[0][:, None]
    ).astype(jnp.float32)
    blocks = obs_weight[0]

    def weigh_obs(values):
        packed = (occupied * values).reshape(blocks.shape[0], blocks.shape[1])
        mixed = jnp.einsum("nij,nj->ni", blocks, packed, precision=lax.Precision.HIGHEST)
        return occupied * mixed.reshape(occupied.shape)

    lane_count = field_shape[-1]
    field_rows = TR * rate_x.size // lane_count
    flat_index = cell_index.reshape(1, -1)
    row_of = flat_index // lane_count
    lane_of = flat_index % lane_count

    def deposit_local(arrived):
        flat_cells = (
            jnp.zeros((TR * rate_x.size,), jnp.float32)
            .at[cell_index.reshape(-1)]
            .add(arrived.reshape(-1))
        )
        return flat_cells.reshape(field_shape)

    def observe(vector):
        picked = pick_cells(vector.reshape(field_rows, lane_count), row_of, lane_of)
        return picked.reshape(cell_index.shape)

    weighted = weigh_obs(innovation[0])
    arrived = lax.all_to_all(weighted, ("gx", "gy"), split_axis=0, concat_axis=0, tiled=True)
    right_side = gather_back(deposit_local(arrived))
    solution = jnp.zeros_like(right_side)
    residual = right_side
    direction = right_side
    norm_now = None
    previous_seen = None
    for iteration in range(ITERS):
        seen, norm_next = exchange(observe(spread(residual)), jnp.sum(residual * residual))
        if iteration == 0:
            direction = residual
        else:
            ratio = norm_next / norm_now
            seen = seen + ratio * previous_seen
            direction = residual + ratio * direction
        norm_now = norm_next
        mixed = weigh_obs(seen)
        returned, curvature = exchange(
            mixed, jnp.sum(direction * direction) + jnp.sum(seen * mixed)
        )
        hessian_dir = direction + gather_back(deposit_local(returned))
        step_length = norm_now / curvature
        solution = solution + step_length * direction
        residual = residual - step_length * hessian_dir
        previous_seen = seen
    return (solution, residual)


def solution(mesh):
    placed = (
        P(None, "gx", "gy"),
        P(None, "gx", "gy"),
        P("gx", "gy"),
        P(("gx", "gy"), None, None),
        P(("gx", "gy"), None),
        P(("gx", "gy"), None, None),
        P(("gx", "gy"), None, None, None),
    )
    return jax.shard_map(
        on_device,
        mesh=mesh,
        in_specs=placed,
        out_specs=(P(None, None, "gx", "gy"), P(None, None, "gx", "gy")),
        check_vma=False,
    )
```

```python
import jax
import jax.numpy as jnp
from jax import lax
from jax.sharding import PartitionSpec as P
from jax.experimental import pallas as pl
from jax.experimental.pallas import tpu as pltpu

TR = 2
ITERS = 2


def shift_along(values, distance, line_axis, reverse, filler):
    length = values.shape[line_axis]
    edge_shape = list(values.shape)
    edge_shape[line_axis] = distance
    edge = jnp.full(tuple(edge_shape), filler, values.dtype)
    if reverse:
        return jnp.concatenate(
            [lax.slice_in_dim(values, distance, length, axis=line_axis), edge], axis=line_axis
        )
    return jnp.concatenate(
        [edge, lax.slice_in_dim(values, 0, length - distance, axis=line_axis)], axis=line_axis
    )


def factor_levels(retention, line_axis, reverse):
    length = retention.shape[line_axis]
    stored = []
    factor = retention
    distance = 1
    while distance < length:
        stored.append(factor)
        factor = factor * shift_along(factor, distance, line_axis, reverse, 1.0)
        distance = distance * 2
    return (stored, factor)


def scan_offsets(stored, forcing, line_axis, reverse):
    distance = 1
    for level_factor in stored:
        forcing = forcing + level_factor * shift_along(forcing, distance, line_axis, reverse, 0.0)
        distance = distance * 2
    return forcing


def make_plan(decay_rate, line_axis, axis_name, periodic):
    retention = jnp.exp(-decay_rate)[None]
    one_minus = -jnp.expm1(-decay_rate)
    scaling = jnp.sqrt(one_minus * (1.0 + jnp.exp(-decay_rate)))
    weight = jnp.sqrt(jnp.sqrt(one_minus))
    length = retention.shape[line_axis]
    forward_stored, prefix = factor_levels(retention, line_axis, False)
    backward_stored, suffix = factor_levels(retention, line_axis, True)
    back_of_prefix = scan_offsets(backward_stored, retention * prefix, line_axis, True)
    totals = jnp.stack(
        [
            lax.index_in_dim(prefix, length - 1, line_axis, keepdims=False),
            lax.index_in_dim(suffix, 0, line_axis, keepdims=False),
            lax.index_in_dim(back_of_prefix, 0, line_axis, keepdims=False),
        ]
    )
    return dict(
        retention=retention,
        gain=scaling * weight,
        gain_out=weight * scaling,
        forward_stored=forward_stored,
        backward_stored=backward_stored,
        prefix=prefix,
        suffix=suffix,
        back_of_prefix=back_of_prefix,
        rate_totals=None,
        totals=totals,
        axis_name=axis_name,
        periodic=periodic,
        line_axis=line_axis,
    )


def carries(got, rate_totals, periodic, axis_name):
    count = got.shape[0]
    offsets = [got[k, 0] for k in range(count)]
    back_parts = [got[k, 1] for k in range(count)]
    factors = [rate_totals[k, 0] for k in range(count)]
    back_factors = [rate_totals[k, 1] for k in range(count)]
    back_gains = [rate_totals[k, 2] for k in range(count)]
    if periodic:
        total = offsets[0]
        product = factors[0]
        for k in range(1, count):
            total = factors[k] * total + offsets[k]
            product = product * factors[k]
        first = total / (1.0 - product)
    else:
        first = jnp.zeros_like(offsets[0])
    entering = [first]
    for k in range(count - 1):
        entering.append(offsets[k] + factors[k] * entering[k])
    back_totals = [back_parts[k] + entering[k] * back_gains[k] for k in range(count)]
    if periodic:
        total = back_totals[count - 1]
        product = back_factors[count - 1]
        for k in range(count - 2, -1, -1):
            total = back_totals[k] + back_factors[k] * total
            product = product * back_factors[k]
        last = total / (1.0 - product)
    else:
        last = jnp.zeros_like(offsets[0])
    leaving = [None] * count
    leaving[count - 1] = last
    for k in range(count - 2, -1, -1):
        leaving[k] = back_totals[k + 1] + back_factors[k + 1] * leaving[k + 1]
    place = lax.axis_index(axis_name)
    mine_in = lax.dynamic_index_in_dim(jnp.stack(entering), place, 0, False)
    mine_out = lax.dynamic_index_in_dim(jnp.stack(leaving), place, 0, False)
    return mine_in, mine_out


def line_operator(state_field, plan):
    line_axis = plan["line_axis"]
    length = state_field.shape[line_axis]
    offset = scan_offsets(plan["forward_stored"], plan["gain"] * state_field, line_axis, False)
    back_offset = scan_offsets(
        plan["backward_stored"], plan["retention"] * offset, line_axis, True
    )
    mine = jnp.stack(
        [
            lax.index_in_dim(offset, length - 1, line_axis, keepdims=False),
            lax.index_in_dim(back_offset, 0, line_axis, keepdims=False),
        ]
    )
    if plan["rate_totals"] is None and plan["periodic"]:
        rate_part = plan["totals"].reshape((-1,) + plan["totals"].shape[2:])
        both = lax.all_gather(
            jnp.concatenate([mine.reshape((-1,) + mine.shape[2:]), rate_part]), plan["axis_name"]
        )
        split = mine.shape[0] * mine.shape[1]
        got = both[:, :split].reshape((both.shape[0],) + mine.shape)
        plan["rate_totals"] = both[:, split:].reshape((both.shape[0],) + plan["totals"].shape)
    elif plan["rate_totals"] is None:
        rate_part = jnp.broadcast_to(plan["totals"], (3,) + mine.shape[1:])
        both = lax.all_gather(jnp.concatenate([mine, rate_part]), plan["axis_name"])
        got = both[:, :2]
        plan["rate_totals"] = both[:, 2:, :1]
    else:
        got = lax.all_gather(mine, plan["axis_name"])
    entering, leaving = carries(got, plan["rate_totals"], plan["periodic"], plan["axis_name"])
    entering = jnp.expand_dims(entering, line_axis)
    leaving = jnp.expand_dims(leaving, line_axis)
    forward = offset + plan["prefix"] * entering
    back_offset = back_offset + entering * plan["back_of_prefix"]
    next_factor = shift_along(plan["suffix"], 1, line_axis, True, 1.0)
    next_offset = shift_along(back_offset, 1, line_axis, True, 0.0)
    return plan["gain_out"] * (forward + next_offset + next_factor * leaving)


CHUNK = 512


def split_three(values):
    high = values.astype(jnp.bfloat16)
    rest = values - high.astype(jnp.float32)
    middle = rest.astype(jnp.bfloat16)
    low = (rest - middle.astype(jnp.float32)).astype(jnp.bfloat16)
    return high, middle, low


def pick_kernel(field_ref, rows_ref, lanes_ref, out_ref):
    field_rows, lanes = field_ref.shape
    chunk = rows_ref.shape[1]
    parts = split_three(field_ref[...].T)
    hot = (
        lax.broadcasted_iota(jnp.int32, (field_rows, chunk), 0) == rows_ref[...]
    ).astype(jnp.bfloat16)
    picked = None
    for part in parts:
        term = jnp.dot(part, hot, preferred_element_type=jnp.float32)
        picked = term if picked is None else picked + term
    chosen = lax.broadcasted_iota(jnp.int32, (lanes, chunk), 0) == lanes_ref[...]
    out_ref[...] = jnp.sum(jnp.where(chosen, picked, 0.0), axis=0, keepdims=True)


def pick_cells(field_rows, rows, lanes):
    count = rows.shape[1]
    return pl.pallas_call(
        pick_kernel,
        out_shape=jax.ShapeDtypeStruct((1, count), jnp.float32),
        grid=(count // CHUNK,),
        in_specs=[
            pl.BlockSpec(field_rows.shape, lambda i: (0, 0)),
            pl.BlockSpec((1, CHUNK), lambda i: (0, i)),
            pl.BlockSpec((1, CHUNK), lambda i: (0, i)),
        ],
        out_specs=pl.BlockSpec((1, CHUNK), lambda i: (0, i)),
    )(field_rows, rows, lanes)


def add_kernel(values_ref, rows_ref, lanes_ref, out_ref):
    field_rows, lanes = out_ref.shape
    chunk = rows_ref.shape[1]

    @pl.when(pl.program_id(0) == 0)
    def _():
        out_ref[...] = jnp.zeros_like(out_ref)

    chosen = lax.broadcasted_iota(jnp.int32, (lanes, chunk), 0) == lanes_ref[...]
    placed = jnp.where(chosen, values_ref[...], 0.0)
    hot = (
        lax.broadcasted_iota(jnp.int32, (field_rows, chunk), 0) == rows_ref[...]
    ).astype(jnp.bfloat16)
    total = None
    for part in split_three(placed):
        term = lax.dot_general(
            hot, part, (((1,), (1,)), ((), ())), preferred_element_type=jnp.float32
        )
        total = term if total is None else total + term
    out_ref[...] += total


def add_cells(values, rows, lanes, field_rows, lane_count):
    count = rows.shape[1]
    return pl.pallas_call(
        add_kernel,
        out_shape=jax.ShapeDtypeStruct((field_rows, lane_count), jnp.float32),
        grid=(count // CHUNK,),
        in_specs=[
            pl.BlockSpec((1, CHUNK), lambda i: (0, i)),
            pl.BlockSpec((1, CHUNK), lambda i: (0, i)),
            pl.BlockSpec((1, CHUNK), lambda i: (0, i)),
        ],
        out_specs=pl.BlockSpec((field_rows, lane_count), lambda i: (0, 0)),
        compiler_params=pltpu.CompilerParams(dimension_semantics=("arbitrary",)),
    )(values, rows, lanes)


def exchange(values, partial):
    rows = values.shape[0]
    packed = jnp.concatenate(
        [values, jnp.broadcast_to(partial.astype(values.dtype), (rows, 1))], axis=1
    )
    arrived = lax.all_to_all(packed, ("gx", "gy"), split_axis=0, concat_axis=0, tiled=True)
    return arrived[:, :-1], jnp.sum(arrived[:, -1])


def on_device(rate_x, rate_y, land_mask, obs_cell, obs_count, innovation, obs_weight):
    ocean = land_mask.astype(jnp.float32)
    field_shape = (TR,) + rate_x.shape
    plan_along_x = make_plan(rate_x, 2, "gx", True)
    plan_along_y = make_plan(rate_y, 3, "gy", False)

    def along_x(state_field):
        return line_operator(state_field, plan_along_x)

    def along_y(state_field):
        return line_operator(state_field, plan_along_y)

    def spread(vector):
        return ocean * along_y(along_x(ocean * vector))

    def gather_back(vector):
        return ocean * along_x(along_y(ocean * vector))

    cell_index = obs_cell[0]
    occupied = (
        lax.broadcasted_iota(jnp.int32, cell_index.shape, 1) < obs_count[0][:, None]
    ).astype(jnp.float32)
    blocks = obs_weight[0]

    def weigh_obs(values):
        packed = (occupied * values).reshape(blocks.shape[0], blocks.shape[1])
        mixed = jnp.einsum("nij,nj->ni", blocks, packed, precision=lax.Precision.HIGHEST)
        return occupied * mixed.reshape(occupied.shape)

    lane_count = field_shape[-1]
    field_rows = TR * rate_x.size // lane_count
    flat_index = cell_index.reshape(1, -1)
    row_of = flat_index // lane_count
    lane_of = flat_index % lane_count

    def deposit_local(arrived):
        flat_cells = (
            jnp.zeros((TR * rate_x.size,), jnp.float32)
            .at[cell_index.reshape(-1)]
            .add(arrived.reshape(-1))
        )
        return flat_cells.reshape(field_shape)

    def observe(vector):
        picked = pick_cells(vector.reshape(field_rows, lane_count), row_of, lane_of)
        return picked.reshape(cell_index.shape)

    weighted = weigh_obs(innovation[0])
    arrived = lax.all_to_all(weighted, ("gx", "gy"), split_axis=0, concat_axis=0, tiled=True)
    right_side = gather_back(deposit_local(arrived))
    solution = jnp.zeros_like(right_side)
    residual = right_side
    direction = right_side
    norm_now = None
    previous_seen = None
    for iteration in range(ITERS):
        seen, norm_next = exchange(observe(spread(residual)), jnp.sum(residual * residual))
        if iteration == 0:
            direction = residual
        else:
            ratio = norm_next / norm_now
            seen = seen + ratio * previous_seen
            direction = residual + ratio * direction
        norm_now = norm_next
        mixed = weigh_obs(seen)
        returned, curvature = exchange(
            mixed, jnp.sum(direction * direction) + jnp.sum(seen * mixed)
        )
        hessian_dir = direction + gather_back(deposit_local(returned))
        step_length = norm_now / curvature
        solution = solution + step_length * direction
        residual = residual - step_length * hessian_dir
        previous_seen = seen
    return (solution, residual)


def solution(mesh):
    placed = (
        P(None, "gx", "gy"),
        P(None, "gx", "gy"),
        P("gx", "gy"),
        P(("gx", "gy"), None, None),
        P(("gx", "gy"), None),
        P(("gx", "gy"), None, None),
        P(("gx", "gy"), None, None, None),
    )
    return jax.shard_map(
        on_device,
        mesh=mesh,
        in_specs=placed,
        out_specs=(P(None, None, "gx", "gy"), P(None, None, "gx", "gy")),
        check_vma=False,
    )
```

```python
import jax
import jax.numpy as jnp
from jax import lax
from jax.sharding import PartitionSpec as P
from jax.experimental import pallas as pl
from jax.experimental.pallas import tpu as pltpu

TR = 2
ITERS = 2


def shift_along(values, distance, line_axis, reverse, filler):
    length = values.shape[line_axis]
    edge_shape = list(values.shape)
    edge_shape[line_axis] = distance
    edge = jnp.full(tuple(edge_shape), filler, values.dtype)
    if reverse:
        return jnp.concatenate(
            [lax.slice_in_dim(values, distance, length, axis=line_axis), edge], axis=line_axis
        )
    return jnp.concatenate(
        [edge, lax.slice_in_dim(values, 0, length - distance, axis=line_axis)], axis=line_axis
    )


def factor_levels(retention, line_axis, reverse):
    length = retention.shape[line_axis]
    stored = []
    factor = retention
    distance = 1
    while distance < length:
        stored.append(factor)
        factor = factor * shift_along(factor, distance, line_axis, reverse, 1.0)
        distance = distance * 2
    return (stored, factor)


def scan_offsets(stored, forcing, line_axis, reverse):
    distance = 1
    for level_factor in stored:
        forcing = forcing + level_factor * shift_along(forcing, distance, line_axis, reverse, 0.0)
        distance = distance * 2
    return forcing


def make_plan(decay_rate, line_axis, axis_name, periodic):
    retention = jnp.exp(-decay_rate)[None]
    one_minus = -jnp.expm1(-decay_rate)
    scaling = jnp.sqrt(one_minus * (1.0 + jnp.exp(-decay_rate)))
    weight = jnp.sqrt(jnp.sqrt(one_minus))
    length = retention.shape[line_axis]
    forward_stored, prefix = factor_levels(retention, line_axis, False)
    backward_stored, suffix = factor_levels(retention, line_axis, True)
    back_of_prefix = scan_offsets(backward_stored, retention * prefix, line_axis, True)
    totals = jnp.stack(
        [
            lax.index_in_dim(prefix, length - 1, line_axis, keepdims=False),
            lax.index_in_dim(suffix, 0, line_axis, keepdims=False),
            lax.index_in_dim(back_of_prefix, 0, line_axis, keepdims=False),
        ]
    )
    return dict(
        retention=retention,
        gain=scaling * weight,
        gain_out=weight * scaling,
        forward_stored=forward_stored,
        backward_stored=backward_stored,
        prefix=prefix,
        suffix=suffix,
        back_of_prefix=back_of_prefix,
        rate_totals=lax.all_gather(totals, axis_name) if periodic else None,
        totals=totals,
        axis_name=axis_name,
        periodic=periodic,
        line_axis=line_axis,
    )


def carries(got, rate_totals, periodic, axis_name):
    count = got.shape[0]
    offsets = [got[k, 0] for k in range(count)]
    back_parts = [got[k, 1] for k in range(count)]
    factors = [rate_totals[k, 0] for k in range(count)]
    back_factors = [rate_totals[k, 1] for k in range(count)]
    back_gains = [rate_totals[k, 2] for k in range(count)]
    if periodic:
        total = offsets[0]
        product = factors[0]
        for k in range(1, count):
            total = factors[k] * total + offsets[k]
            product = product * factors[k]
        first = total / (1.0 - product)
    else:
        first = jnp.zeros_like(offsets[0])
    entering = [first]
    for k in range(count - 1):
        entering.append(offsets[k] + factors[k] * entering[k])
    back_totals = [back_parts[k] + entering[k] * back_gains[k] for k in range(count)]
    if periodic:
        total = back_totals[count - 1]
        product = back_factors[count - 1]
        for k in range(count - 2, -1, -1):
            total = back_totals[k] + back_factors[k] * total
            product = product * back_factors[k]
        last = total / (1.0 - product)
    else:
        last = jnp.zeros_like(offsets[0])
    leaving = [None] * count
    leaving[count - 1] = last
    for k in range(count - 2, -1, -1):
        leaving[k] = back_totals[k + 1] + back_factors[k + 1] * leaving[k + 1]
    place = lax.axis_index(axis_name)
    mine_in = lax.dynamic_index_in_dim(jnp.stack(entering), place, 0, False)
    mine_out = lax.dynamic_index_in_dim(jnp.stack(leaving), place, 0, False)
    return mine_in, mine_out


def line_operator(state_field, plan):
    line_axis = plan["line_axis"]
    length = state_field.shape[line_axis]
    offset = scan_offsets(plan["forward_stored"], plan["gain"] * state_field, line_axis, False)
    back_offset = scan_offsets(
        plan["backward_stored"], plan["retention"] * offset, line_axis, True
    )
    mine = jnp.stack(
        [
            lax.index_in_dim(offset, length - 1, line_axis, keepdims=False),
            lax.index_in_dim(back_offset, 0, line_axis, keepdims=False),
        ]
    )
    if plan["rate_totals"] is None:
        rate_part = jnp.broadcast_to(plan["totals"], (3,) + mine.shape[1:])
        both = lax.all_gather(jnp.concatenate([mine, rate_part]), plan["axis_name"])
        got = both[:, :2]
        plan["rate_totals"] = both[:, 2:, :1]
    else:
        got = lax.all_gather(mine, plan["axis_name"])
    entering, leaving = carries(got, plan["rate_totals"], plan["periodic"], plan["axis_name"])
    entering = jnp.expand_dims(entering, line_axis)
    leaving = jnp.expand_dims(leaving, line_axis)
    forward = offset + plan["prefix"] * entering
    back_offset = back_offset + entering * plan["back_of_prefix"]
    next_factor = shift_along(plan["suffix"], 1, line_axis, True, 1.0)
    next_offset = shift_along(back_offset, 1, line_axis, True, 0.0)
    return plan["gain_out"] * (forward + next_offset + next_factor * leaving)


CHUNK = 4096


def split_three(values):
    high = values.astype(jnp.bfloat16)
    rest = values - high.astype(jnp.float32)
    middle = rest.astype(jnp.bfloat16)
    low = (rest - middle.astype(jnp.float32)).astype(jnp.bfloat16)
    return high, middle, low


def pick_kernel(field_ref, rows_ref, lanes_ref, out_ref):
    field_rows, lanes = field_ref.shape
    chunk = rows_ref.shape[1]
    parts = split_three(field_ref[...].T)
    hot = (
        lax.broadcasted_iota(jnp.int32, (field_rows, chunk), 0) == rows_ref[...]
    ).astype(jnp.bfloat16)
    picked = None
    for part in parts:
        term = jnp.dot(part, hot, preferred_element_type=jnp.float32)
        picked = term if picked is None else picked + term
    chosen = lax.broadcasted_iota(jnp.int32, (lanes, chunk), 0) == lanes_ref[...]
    out_ref[...] = jnp.sum(jnp.where(chosen, picked, 0.0), axis=0, keepdims=True)


def pick_cells(field_rows, rows, lanes):
    count = rows.shape[1]
    return pl.pallas_call(
        pick_kernel,
        out_shape=jax.ShapeDtypeStruct((1, count), jnp.float32),
        grid=(count // CHUNK,),
        in_specs=[
            pl.BlockSpec(field_rows.shape, lambda i: (0, 0)),
            pl.BlockSpec((1, CHUNK), lambda i: (0, i)),
            pl.BlockSpec((1, CHUNK), lambda i: (0, i)),
        ],
        out_specs=pl.BlockSpec((1, CHUNK), lambda i: (0, i)),
    )(field_rows, rows, lanes)


def add_kernel(values_ref, rows_ref, lanes_ref, out_ref):
    field_rows, lanes = out_ref.shape
    chunk = rows_ref.shape[1]

    @pl.when(pl.program_id(0) == 0)
    def _():
        out_ref[...] = jnp.zeros_like(out_ref)

    chosen = lax.broadcasted_iota(jnp.int32, (lanes, chunk), 0) == lanes_ref[...]
    placed = jnp.where(chosen, values_ref[...], 0.0)
    hot = (
        lax.broadcasted_iota(jnp.int32, (field_rows, chunk), 0) == rows_ref[...]
    ).astype(jnp.bfloat16)
    total = None
    for part in split_three(placed):
        term = lax.dot_general(
            hot, part, (((1,), (1,)), ((), ())), preferred_element_type=jnp.float32
        )
        total = term if total is None else total + term
    out_ref[...] += total


def add_cells(values, rows, lanes, field_rows, lane_count):
    count = rows.shape[1]
    return pl.pallas_call(
        add_kernel,
        out_shape=jax.ShapeDtypeStruct((field_rows, lane_count), jnp.float32),
        grid=(count // CHUNK,),
        in_specs=[
            pl.BlockSpec((1, CHUNK), lambda i: (0, i)),
            pl.BlockSpec((1, CHUNK), lambda i: (0, i)),
            pl.BlockSpec((1, CHUNK), lambda i: (0, i)),
        ],
        out_specs=pl.BlockSpec((field_rows, lane_count), lambda i: (0, 0)),
        compiler_params=pltpu.CompilerParams(dimension_semantics=("arbitrary",)),
    )(values, rows, lanes)


def exchange(values, partial):
    rows = values.shape[0]
    packed = jnp.concatenate(
        [values, jnp.broadcast_to(partial.astype(values.dtype), (rows, 1))], axis=1
    )
    arrived = lax.all_to_all(packed, ("gx", "gy"), split_axis=0, concat_axis=0, tiled=True)
    return arrived[:, :-1], jnp.sum(arrived[:, -1])


def on_device(rate_x, rate_y, land_mask, obs_cell, obs_count, innovation, obs_weight):
    ocean = land_mask.astype(jnp.float32)
    field_shape = (TR,) + rate_x.shape
    plan_along_x = make_plan(rate_x, 2, "gx", True)
    plan_along_y = make_plan(rate_y, 3, "gy", False)

    def along_x(state_field):
        return line_operator(state_field, plan_along_x)

    def along_y(state_field):
        return line_operator(state_field, plan_along_y)

    def spread(vector):
        return ocean * along_y(along_x(ocean * vector))

    def gather_back(vector):
        return ocean * along_x(along_y(ocean * vector))

    cell_index = obs_cell[0]
    occupied = (
        lax.broadcasted_iota(jnp.int32, cell_index.shape, 1) < obs_count[0][:, None]
    ).astype(jnp.float32)
    blocks = obs_weight[0]

    def weigh_obs(values):
        packed = (occupied * values).reshape(blocks.shape[0], blocks.shape[1])
        mixed = jnp.einsum("nij,nj->ni", blocks, packed, precision=lax.Precision.HIGHEST)
        return occupied * mixed.reshape(occupied.shape)

    lane_count = field_shape[-1]
    field_rows = TR * rate_x.size // lane_count
    flat_index = cell_index.reshape(1, -1)
    row_of = flat_index // lane_count
    lane_of = flat_index % lane_count

    def deposit_local(arrived):
        flat_cells = (
            jnp.zeros((TR * rate_x.size,), jnp.float32)
            .at[cell_index.reshape(-1)]
            .add(arrived.reshape(-1))
        )
        return flat_cells.reshape(field_shape)

    def observe(vector):
        picked = pick_cells(vector.reshape(field_rows, lane_count), row_of, lane_of)
        return picked.reshape(cell_index.shape)

    weighted = weigh_obs(innovation[0])
    arrived = lax.all_to_all(weighted, ("gx", "gy"), split_axis=0, concat_axis=0, tiled=True)
    right_side = gather_back(deposit_local(arrived))
    solution = jnp.zeros_like(right_side)
    residual = right_side
    direction = right_side
    norm_now = None
    previous_seen = None
    for iteration in range(ITERS):
        seen, norm_next = exchange(observe(spread(residual)), jnp.sum(residual * residual))
        if iteration == 0:
            direction = residual
        else:
            ratio = norm_next / norm_now
            seen = seen + ratio * previous_seen
            direction = residual + ratio * direction
        norm_now = norm_next
        mixed = weigh_obs(seen)
        returned, curvature = exchange(
            mixed, jnp.sum(direction * direction) + jnp.sum(seen * mixed)
        )
        hessian_dir = direction + gather_back(deposit_local(returned))
        step_length = norm_now / curvature
        solution = solution + step_length * direction
        residual = residual - step_length * hessian_dir
        previous_seen = seen
    return (solution, residual)


def solution(mesh):
    placed = (
        P(None, "gx", "gy"),
        P(None, "gx", "gy"),
        P("gx", "gy"),
        P(("gx", "gy"), None, None),
        P(("gx", "gy"), None),
        P(("gx", "gy"), None, None),
        P(("gx", "gy"), None, None, None),
    )
    return jax.shard_map(
        on_device,
        mesh=mesh,
        in_specs=placed,
        out_specs=(P(None, None, "gx", "gy"), P(None, None, "gx", "gy")),
        check_vma=False,
    )
```
